32 devices in a mesh: grp: 2 (over x), beam: 16 (over z, y, core).
Axes of the slice: x: 2, y: 2, z: 4, core: 2. Of those that a mesh axis runs over, the one named last changes fastest.
Arguments:
- s_matrix: bfloat16 [2, 2048, 16, 4096], P(None, ('grp', 'beam')), parts along dimension 1, may hold values from -6 to 6
- beam_weight: float32 [2, 2048], P(None, ('grp', 'beam')), parts along dimension 1, may hold values from -0.25 to 0.25
- probe_shift: int32 [256, 2], P(('grp', 'beam')), parts along dimension 0, may hold values from 0 to 191
- probe_cutoff: int32 [256], P(('grp', 'beam')), parts along dimension 0, may hold values from 64 to 512
- target: bfloat16 [2, 256, 4096], P(None, ('grp', 'beam')), parts along dimension 1, may hold values from -3 to 3
- target_exp: int32 [256], P(('grp', 'beam')), parts along dimension 0, may hold values from -1 to 2
Outputs:
- s_grad: bfloat16 [2, 2048, 16, 4096], P(None, ('grp', 'beam')), parts along dimension 1
The draws below stay inside these ranges and needn't reach their ends.
There are 2 independent parts, one for each index of `grp`. The reference program is written for one: setup_inputs(seed, part) draws one part's arguments, and reference() takes and returns one part's arrays. A program takes and returns all parts, laid end to end along the dimension named above; each array names one. Nothing has to cross between parts.
All inputs are finite; a program needn't handle non-finite values.
Results may differ from the reference program's by a relative error of at most 0.006.
Values may be sent and summed in bfloat16 or wider, within the bound.
A program may use at most 128 MiB of HBM per device.

```python
import math
import jax
import jax.numpy as jnp
from jax import lax

SIDE = 32
BEAMS = 1024
PIX = 4096
GRID = 192
TILE_SIDE = 4
TILES = 16
PROBES = 128


def set_ends(array, own_key, smallest, top_value):
    extent = array.shape
    spot = [jax.random.randint(jax.random.fold_in(own_key, axis), (), 0, extent[axis]) for axis in range(len(extent))]
    array = array.at[tuple(spot)].set(smallest)
    longest = extent.index(max(extent))
    spot[longest] = (spot[longest] + 1) % extent[longest]
    return array.at[tuple(spot)].set(top_value)


def levels(stream_key, dims, split, smallest, top_value):
    loudness, own = 1.0, jax.random.fold_in(stream_key, 6)
    for axis_at, blocks in split:
        heights = jnp.exp(jax.random.uniform(jax.random.fold_in(own, axis_at), (blocks,), jnp.float32, smallest / len(split), top_value / len(split)))
        loudness = loudness * jnp.repeat(heights, dims[axis_at] // blocks).reshape([-1 if axis == axis_at else 1 for axis in range(len(dims))])
    return loudness


def bell_draw(own_key, shape, spread, most, split=(), kind=jnp.bfloat16):
    array = jax.random.normal(own_key, shape, jnp.float32) * spread
    if len(split) > 0:
        array = levels(own_key, shape, split, -0.22, 0.18) * array
    return jnp.clip(array, min=-most, max=most).astype(kind)


def setup_inputs(seed: int = 0, part: int = 0) -> dict:
    streams_of = jax.random.split(jax.random.key(seed), 7)
    own_keys = jax.random.split(jax.random.fold_in(streams_of[6], part), 7)
    s_matrix = bell_draw(own_keys[0], (2, BEAMS, TILES, PIX), 1.0, 6.0, ((1, 16),))
    beam_weight = bell_draw(own_keys[1], (2, BEAMS), (BEAMS // 2) ** -0.5, 0.25, ((1, 16),), jnp.float32)
    probe_shift = set_ends(jax.random.randint(own_keys[2], (PROBES, 2), 0, GRID), jax.random.fold_in(own_keys[2], 1), 0, GRID - 1).astype(jnp.int32)
    probe_cutoff = set_ends(jax.random.randint(own_keys[3], (PROBES,), BEAMS // 16, BEAMS // 2 + 1), jax.random.fold_in(own_keys[3], 1), BEAMS // 16, (BEAMS // 2 + 1) - 1).astype(jnp.int32)
    target = bell_draw(own_keys[4], (2, PROBES, PIX), 0.5, 3.0, ((1, 16),))
    target_exp = set_ends(jax.random.randint(own_keys[5], (PROBES,), -1, 3), jax.random.fold_in(own_keys[5], 1), -1, 2).astype(jnp.int32)
    return dict(s_matrix=s_matrix, beam_weight=beam_weight, probe_shift=probe_shift, probe_cutoff=probe_cutoff, target=target, target_exp=target_exp)


TWO_PI = 2.0 * math.pi

def window_of(shift):
    step = GRID // TILE_SIDE
    return shift[:, 0] // step * TILE_SIDE + shift[:, 1] // step

def coefficients(beam_index, weight, shift, cutoff):
    half = SIDE // 2
    freq_x = beam_index % SIDE - half
    freq_y = beam_index // SIDE - half
    ramp = (freq_x[None, :] * shift[:, 0:1] + freq_y[None, :] * shift[:, 1:2]) % GRID
    phase = ramp.astype(jnp.float32) * (TWO_PI / GRID)
    inside = (freq_x * freq_x + freq_y * freq_y)[None, :] <= cutoff[:, None]
    cosine = jnp.cos(phase)
    sine = jnp.sin(phase)
    w_real = weight[0][None, :]
    w_imag = weight[1][None, :]
    c_real = jnp.where(inside, w_real * cosine + w_imag * sine, 0.0)
    c_imag = jnp.where(inside, w_imag * cosine - w_real * sine, 0.0)
    return (c_real.astype(jnp.bfloat16), c_imag.astype(jnp.bfloat16))

def reference(s_matrix, beam_weight, probe_shift, probe_cutoff, target, target_exp):
    group = 32
    count = BEAMS // group
    s_blocks = s_matrix.reshape(2, count, group, TILES, PIX).transpose(1, 0, 2, 3, 4)
    w_blocks = beam_weight.reshape(2, count, group).transpose(1, 0, 2)
    starts = jnp.arange(count, dtype=jnp.int32) * group
    windows = window_of(probe_shift)
    onehot = windows[:, None] == jnp.arange(TILES, dtype=jnp.int32)[None, :]

    def expand(start, weight):
        index = start + jnp.arange(group, dtype=jnp.int32)
        c_real, c_imag = coefficients(index, weight, probe_shift, probe_cutoff)
        zero = jnp.zeros((), jnp.bfloat16)
        e_real = jnp.where(onehot[:, None, :], c_real[:, :, None], zero).reshape(PROBES, group * TILES)
        e_imag = jnp.where(onehot[:, None, :], c_imag[:, :, None], zero).reshape(PROBES, group * TILES)
        return (e_real, e_imag)

    def add_wave(total, item):
        start, block, weight = item
        e_real, e_imag = expand(start, weight)
        s_re = block[0].reshape(group * TILES, PIX)
        s_im = block[1].reshape(group * TILES, PIX)
        w_re = jnp.dot(e_real, s_re, preferred_element_type=jnp.float32) - jnp.dot(e_imag, s_im, preferred_element_type=jnp.float32)
        w_im = jnp.dot(e_real, s_im, preferred_element_type=jnp.float32) + jnp.dot(e_imag, s_re, preferred_element_type=jnp.float32)
        return ((total[0] + w_re, total[1] + w_im), None)
    empty = jnp.zeros((PROBES, PIX), jnp.float32)
    (wave_re, wave_im), _ = lax.scan(add_wave, (empty, empty), (starts, s_blocks, w_blocks))
    scale = jnp.exp2(target_exp.astype(jnp.float32))[None, :, None]
    scaled = target.astype(jnp.float32) * scale
    residual = (jnp.stack([wave_re, wave_im]) - scaled).astype(jnp.bfloat16)

    def grad(item):
        start, weight = item
        e_real, e_imag = expand(start, weight)
        g_re = jnp.dot(e_real.T, residual[0], preferred_element_type=jnp.float32) + jnp.dot(e_imag.T, residual[1], preferred_element_type=jnp.float32)
        g_im = jnp.dot(e_real.T, residual[1], preferred_element_type=jnp.float32) - jnp.dot(e_imag.T, residual[0], preferred_element_type=jnp.float32)
        return jnp.stack([g_re, g_im]).reshape(2, group, TILES, PIX).astype(jnp.bfloat16)
    blocks = lax.map(grad, (starts, w_blocks))
    return blocks.transpose(1, 0, 2, 3, 4).reshape(2, BEAMS, TILES, PIX)
```

```python
import functools
import math

import jax
import jax.numpy as jnp
from jax import lax
from jax.experimental import pallas as pl
from jax.experimental.pallas import tpu as pltpu
from jax.sharding import PartitionSpec as P

SIDE = 32
GRID = 192
TILE_SIDE = 4
TWO_PI = 2.0 * math.pi
CHUNKS = 8
SWAP = True
GAP_NEAR = 2
GAP_FAR = 4
MATMUL_COLUMNS = 512


KINDS = ("YY",) * 8
LINK_RATE = 46.5e3
CORE_RATE = 250e3
LINK_LAG = 1.66
CORE_LAG = 0.9
PRODUCT_US = 5.5
ADD_US = 0.3
NAMES = ("r1", "r2", "r3f", "r3n", "r4", "ga", "gb", "gn1", "gn2", "gf1", "gf2", "ac")


def steps_of(inner, kind):
    sums, spread = kind
    steps = [("M", (), (("c", "r1", 4),), 0, ())]
    if spread == "Y":
        first = (("m", "gf1", 1), ("o", "gn1", 1), ("y", "ga", 1))
    else:
        first = (("y", "ga", 1), ("m", "gf1", 1), ("o", "gn1", 1))
    edge_sums = (("t", "r3f", 1), ("t", "r3n", 1)) if sums == "Y" else (("t", "r3f", 2), ("t", "r3n", 2))
    if sums == "Y":
        steps.append(("C", ("r1",), (("y", "r2", 2),), 4, ("M",)))
        if inner:
            steps.append(("Y", ("r2",), (), 2, ("C",)))
            steps.append(("F", ("r3f",), (("m", "r4", 1),), 1, ("Y",)))
            steps.append(("N", ("r3n", "r4"), first, 1, ("F",)))
        else:
            steps.append(("Y", ("r2",), edge_sums, 2, ("C",)))
        last = "N"
    else:
        if inner:
            steps.append(("C", ("r1",), (), 4, ("M",)))
            steps.append(("F", ("r3f",), (("m", "r4", 2),), 2, ("C",)))
            steps.append(("N", ("r3n", "r4"), (("y", "r2", 1),), 2, ("F",)))
            steps.append(("Y", ("r2",), first, 1, ("N",)))
        else:
            steps.append(("C", ("r1",), edge_sums, 4, ("M",)))
        last = "Y"
    if spread == "Y":
        if inner:
            steps.append(("G1", ("gf1",), (("o", "gf1", 1), ("y", "gb", 1)), 0, ()))
            steps.append(("A", ("ga", "gb"), (("c", "ac", 4),), 0, (last, "G1")))
        else:
            steps.append(("G1", ("gn1",), (("y", "ga", 1),), 0, ()))
            steps.append(("G2", ("gf1",), (("y", "gb", 1),), 0, ()))
            steps.append(("A", ("ga", "gb"), (("c", "ac", 4),), 0, ("G1", "G2")))
    elif inner:
        steps.append(("H", ("ga",), (("m", "gf2", 1), ("o", "gn2", 1)), 0, ()))
        steps.append(("G1", ("gf1",), (("o", "gf1", 1),), 0, ()))
        steps.append(("A", ("gf2",), (("o", "gf2", 1), ("c", "ac", 4)), 0, (last, "H", "G1")))
    else:
        steps.append(("A", ("gn1", "gn2", "gf1", "gf2"), (("c", "ac", 4),), 0, ()))
    steps.append(("E", ("ac",), (), 0, ()))
    return steps


def schedule(block_bytes):
    chunks = len(KINDS)
    waiting = [[(k, step) for k in range(chunks) for step in steps_of(inner, KINDS[k])] for inner in (False, True)]
    arrived, done = ({}, {}), ({}, {})
    free, links = [0.0, 0.0], {}
    order = ([], [])
    while waiting[0] or waiting[1]:
        best = None
        for role in (0, 1):
            for k, step in waiting[role]:
                name, needs, _, _, after = step
                if name == "M" and k > 0 and (k - 1, "M") not in done[role]:
                    continue
                if any((k, x) not in arrived[role] for x in needs) or any((k, x) not in done[role] for x in after):
                    continue
                ready = max([free[role]] + [arrived[role][k, x] for x in needs])
                rank = (ready, name == "M", k, role, name)
                if best is None or rank < best[0]:
                    best = (rank, role, k, step)
        (ready, *_), role, k, step = best
        name, _, sends, blocks, _ = step
        end = ready + (PRODUCT_US if name == "M" else 0.02 * chunks + ADD_US * blocks) / chunks
        free[role] = end
        done[role][k, name] = end
        waiting[role].remove((k, step))
        order[role].append((k, name))
        for link, message, count in sends:
            rate, lag = (CORE_RATE, CORE_LAG) if link == "c" else (LINK_RATE, LINK_LAG)
            sent = max(end, links.get((role, link), 0.0)) + count * block_bytes / rate
            links[role, link] = sent
            arrived[{"t": 1, "o": 0}.get(link, role)][k, message] = sent + lag
    return order


def grid_kernel(
    n, local, tile_count, pixels,
    par_ref, weight_ref, target_ref, s_ref,
    res_ref, left_ref,
    pars, s_vmem, acc, sbuf, r1, r2, r3, r4,
    par_send, par_recv, s_sem, send_sem, recv_sem,
):
    me = lax.axis_index("beam")
    unit = par_ref.shape[0]
    rows = n * unit
    width = local * tile_count
    chunks = len(KINDS)
    wide = pixels // chunks
    block = rows // 8
    core, across, line = me % 2, me // 2 % 2, me // 4
    side = line // 2
    far = 1 - side
    inward = (1 - 2 * side) * 4
    peers = {
        "c": me + 1 - 2 * core,
        "y": me + 2 - 4 * across,
        "t": me + inward,
        "m": me + inward,
        "o": me - inward,
    }

    def columns(k):
        return pl.ds(k * wide, wide)

    loads = []
    for k in range(chunks):
        load = pltpu.make_async_copy(s_ref.at[:, columns(k)], s_vmem.at[:, columns(k)], s_sem.at[k])
        load.start()
        loads.append(load)

    barrier = pltpu.get_barrier_semaphore()
    for ahead in range(1, n):
        pl.semaphore_signal(
            barrier, inc=1, device_id={"beam": lax.rem(me + ahead, n)}, device_id_type=pl.DeviceIdType.MESH
        )
    pl.semaphore_wait(barrier, n - 1)

    def remote(source, target, send_semaphore, recv_semaphore, peer):
        return pltpu.make_async_remote_copy(
            src_ref=source,
            dst_ref=target,
            send_sem=send_semaphore,
            recv_sem=recv_semaphore,
            device_id={"beam": peer},
            device_id_type=pl.DeviceIdType.MESH,
        )

    mine = pl.ds(pl.multiple_of(me * unit, unit), unit)
    pars[mine, :] = par_ref[...]
    asked = [
        remote(par_ref, pars.at[mine, :], par_send.at[ahead - 1], par_recv.at[ahead - 1], lax.rem(me + ahead, n))
        for ahead in range(1, n)
    ]
    for copy in asked:
        copy.start()
    for copy in asked:
        copy.wait_recv()

    half = SIDE // 2
    beam = me * local + lax.broadcasted_iota(jnp.int32, (1, local), 1)
    freq_x = beam % SIDE - half
    freq_y = beam // SIDE - half
    shift_x = pars[:, 0:1]
    shift_y = pars[:, 1:2]
    cutoff = pars[:, 2:3]
    ramp = (freq_x * shift_x + freq_y * shift_y) % GRID
    phase = ramp.astype(jnp.float32) * (TWO_PI / GRID)
    inside = (freq_x * freq_x + freq_y * freq_y) <= cutoff
    cosine = jnp.cos(phase)
    sine = jnp.sin(phase)
    w_real = weight_ref[0:1, :]
    w_imag = weight_ref[1:2, :]
    c_real = jnp.where(inside, w_real * cosine + w_imag * sine, 0.0)
    c_imag = jnp.where(inside, w_imag * cosine - w_real * sine, 0.0)
    is_real = lax.broadcasted_iota(jnp.int32, (rows, 1), 0) % unit < unit // 2
    first = jnp.where(is_real, c_real, c_imag).astype(jnp.bfloat16)
    second = jnp.where(is_real, -c_imag, c_real).astype(jnp.bfloat16)
    step = GRID // TILE_SIDE
    window = shift_x // step * TILE_SIDE + shift_y // step
    place_of = lax.broadcasted_iota(jnp.int32, (1, width), 1)
    chosen = window == place_of % tile_count
    spread = lax.broadcasted_iota(jnp.int32, (local, width), 1) // tile_count
    spread = (spread == lax.broadcasted_iota(jnp.int32, (local, width), 0)).astype(jnp.float32).astype(jnp.bfloat16)
    for at, part in ((0, first), (width, second)):
        full = jnp.dot(part, spread, preferred_element_type=jnp.float32)
        left_ref[:, at : at + width] = jnp.where(chosen, full, 0.0).astype(jnp.bfloat16)

    own = (me * unit // block // 4, me * unit // block // 2 % 2, me * unit // block % 2)
    own_rows = pl.ds(pl.multiple_of(me * unit % block, unit), unit)

    def run(inner, steps):
        sent = []

        def send(k, link, message, source, target):
            copy = remote(
                source, target, send_sem.at[k, len([1 for other, _ in sent if other == k])],
                recv_sem.at[k, NAMES.index(message)], peers[link],
            )
            copy.start()
            sent.append((k, copy))

        def got(k, message, view):
            remote(view, view, send_sem.at[k, 0], recv_sem.at[k, NAMES.index(message)], peers["c"]).wait_recv()

        def low(x):
            return x.astype(jnp.bfloat16)

        def spread_first(k):
            held = res_ref.at[k, core, across, side]
            if KINDS[k][1] == "Y":
                send(k, "m", "gf1", held, held)
                send(k, "o", "gn1", held, held)
                send(k, "y", "ga", held, held)
            else:
                send(k, "y", "ga", held, held)
                send(k, "m", "gf1", held, held)
                send(k, "o", "gn1", held, held)

        def take(k, name):
            by_y = KINDS[k][0] == "Y"
            at = (k, core, across)
            here = (k, core, across, side)
            if name == "M":
                loads[k].wait()
                product = jnp.dot(left_ref[...], s_vmem[:, columns(k)], preferred_element_type=jnp.float32)
                acc[k] = product.reshape(2, 2, 2, block, wide)
                goal = target_ref[:, columns(k)].astype(jnp.float32) * jnp.exp2(par_ref[:, 3:4].astype(jnp.float32))
                acc[(k, *own, own_rows)] = acc[(k, *own, own_rows)] - goal
                sbuf[k, 1 - core] = low(acc[k, 1 - core])
                send(k, "c", "r1", sbuf.at[k, 1 - core], r1.at[k])
            elif name == "C":
                got(k, "r1", r1.at[k])
                if by_y:
                    sbuf[k, core, 1 - across] = low(acc[k, core, 1 - across] + r1[k, 1 - across].astype(jnp.float32))
                    send(k, "y", "r2", sbuf.at[k, core, 1 - across], r2.at[k])
                    acc[at] = acc[at] + r1[k, across].astype(jnp.float32)
                elif inner:
                    acc[k, core] = acc[k, core] + r1[k].astype(jnp.float32)
                else:
                    for at_side, message, slot in ((far, "r3f", 0), (side, "r3n", 1)):
                        total = acc[k, core, :, at_side] + r1[k, :, at_side].astype(jnp.float32)
                        sbuf[k, core, :, at_side] = low(total)
                        send(k, "t", message, sbuf.at[k, core, :, at_side], r3.at[k, slot])
            elif name == "Y":
                if by_y:
                    got(k, "r2", r2.at[k])
                    total = acc[at] + r2[k].astype(jnp.float32)
                    if inner:
                        acc[at] = total
                    else:
                        sbuf[at] = low(total)
                        send(k, "t", "r3f", sbuf.at[(*at, far)], r3.at[k, 0, 0])
                        send(k, "t", "r3n", sbuf.at[(*at, side)], r3.at[k, 1, 0])
                else:
                    got(k, "r2", r2.at[k, 0])
                    res_ref[here] = low(acc[here] + r2[k, 0].astype(jnp.float32))
                    spread_first(k)
            elif name == "F":
                if by_y:
                    got(k, "r3f", r3.at[k, 0, 0])
                    sbuf[(*at, far)] = low(acc[(*at, far)] + r3[k, 0, 0].astype(jnp.float32))
                    send(k, "m", "r4", sbuf.at[(*at, far)], r4.at[k, 0])
                else:
                    got(k, "r3f", r3.at[k, 0])
                    sbuf[k, core, :, far] = low(acc[k, core, :, far] + r3[k, 0].astype(jnp.float32))
                    send(k, "m", "r4", sbuf.at[k, core, :, far], r4.at[k])
            elif name == "N":
                if by_y:
                    got(k, "r3n", r3.at[k, 1, 0])
                    got(k, "r4", r4.at[k, 0])
                    total = acc[here] + r3[k, 1, 0].astype(jnp.float32) + r4[k, 0].astype(jnp.float32)
                    res_ref[here] = low(total)
                    spread_first(k)
                else:
                    got(k, "r3n", r3.at[k, 1])
                    got(k, "r4", r4.at[k])
                    there = (k, core, 1 - across, side)
                    total = acc[there] + r3[k, 1, 1 - across].astype(jnp.float32) + r4[k, 1 - across].astype(jnp.float32)
                    sbuf[there] = low(total)
                    send(k, "y", "r2", sbuf.at[there], r2.at[k, 0])
                    acc[here] = acc[here] + r3[k, 1, across].astype(jnp.float32) + r4[k, across].astype(jnp.float32)
            elif name == "A":
                if KINDS[k][1] == "Y":
                    got(k, "ga", res_ref.at[here])
                    got(k, "gb", res_ref.at[here])
                elif inner:
                    got(k, "gf2", res_ref.at[here])
                    held = res_ref.at[k, core, 1 - across, far]
                    send(k, "o", "gf2", held, held)
                else:
                    for message in ("gn1", "gn2", "gf1", "gf2"):
                        got(k, message, res_ref.at[here])
                send(k, "c", "ac", res_ref.at[k, core], res_ref.at[k, core])
            elif name == "H":
                got(k, "ga", res_ref.at[here])
                held = res_ref.at[k, core, 1 - across, side]
                send(k, "m", "gf2", held, held)
                send(k, "o", "gn2", held, held)
            elif name == "G1":
                if inner:
                    got(k, "gf1", res_ref.at[here])
                    held = res_ref.at[(*at, far)]
                    send(k, "o", "gf1", held, held)
                    if KINDS[k][1] == "Y":
                        send(k, "y", "gb", held, held)
                else:
                    got(k, "gn1", res_ref.at[here])
                    held = res_ref.at[here]
                    send(k, "y", "ga", held, held)
            elif name == "G2":
                got(k, "gf1", res_ref.at[here])
                held = res_ref.at[(*at, far)]
                send(k, "y", "gb", held, held)
            elif name == "E":
                got(k, "ac", res_ref.at[k, 1 - core])

        for k, name in steps:
            take(k, name)
        for _, copy in sent:
            copy.wait_send()

    edge_steps, inner_steps = schedule(block * wide * 2)
    middle = (line == 1) | (line == 2)

    @pl.when(middle)
    def _():
        run(True, inner_steps)

    @pl.when(jnp.logical_not(middle))
    def _():
        run(False, edge_steps)

    for copy in asked:
        copy.wait_send()


def stage_strides(n):
    return [2**k for k in range(n.bit_length() - 1)]


def orders(n):
    strides = stage_strides(n)
    other = list(strides)
    if SWAP and len(other) > 2:
        other[1], other[2] = other[2], other[1]
    return strides, other


def place(me, strides, unit, upto):
    levels = len(strides)
    base = 0
    for k in range(upto):
        base = base + (me // strides[k]) % 2 * (unit * 2 ** (levels - 1 - k))
    return base


def wave_kernel(
    n, local, tile_count, pixels, strides, other,
    par_ref, weight_ref, target_ref, s_ref,
    res_ref, left_ref,
    pars, s_vmem, acc, sbuf, rbuf, mixed_left, mixed_res,
    par_send, par_recv, s_sem, send_sem, recv_sem,
):
    levels = len(strides)
    me = lax.axis_index("beam")
    unit = par_ref.shape[0]
    rows = n * unit
    width = local * tile_count
    wide = pixels // CHUNKS

    def order(c):
        return other if c % 2 else strides

    moves = [(place(i, other, unit, levels), place(i, strides, unit, levels)) for i in range(n)]

    def partner(stride):
        return me + (1 - 2 * ((me // stride) % 2)) * stride

    def columns(c):
        return pl.ds(c * wide, wide)

    loads = []
    for c in range(CHUNKS):
        load = pltpu.make_async_copy(s_ref.at[:, columns(c)], s_vmem.at[:, columns(c)], s_sem.at[c])
        load.start()
        loads.append(load)

    barrier = pltpu.get_barrier_semaphore()
    for ahead in range(1, n):
        pl.semaphore_signal(
            barrier, inc=1, device_id={"beam": lax.rem(me + ahead, n)}, device_id_type=pl.DeviceIdType.MESH
        )
    pl.semaphore_wait(barrier, n - 1)

    sent = []

    def send(source, target, send_semaphore, recv_semaphore, peer):
        copy = pltpu.make_async_remote_copy(
            src_ref=source,
            dst_ref=target,
            send_sem=send_semaphore,
            recv_sem=recv_semaphore,
            device_id={"beam": peer},
            device_id_type=pl.DeviceIdType.MESH,
        )
        copy.start()
        sent.append(copy)
        return copy

    def mine(k, steps=strides):
        size = unit * 2 ** (levels - k)
        return pl.ds(pl.multiple_of(place(me, steps, unit, k), size), size)

    pars[mine(levels), :] = par_ref[...]
    asked = [
        send(par_ref, pars.at[mine(levels), :], par_send.at[ahead - 1], par_recv.at[ahead - 1], lax.rem(me + ahead, n))
        for ahead in range(1, n)
    ]
    for copy in asked:
        copy.wait_recv()

    half = SIDE // 2
    beam = me * local + lax.broadcasted_iota(jnp.int32, (1, local), 1)
    freq_x = beam % SIDE - half
    freq_y = beam // SIDE - half
    shift_x = pars[:, 0:1]
    shift_y = pars[:, 1:2]
    cutoff = pars[:, 2:3]
    ramp = (freq_x * shift_x + freq_y * shift_y) % GRID
    phase = ramp.astype(jnp.float32) * (TWO_PI / GRID)
    inside = (freq_x * freq_x + freq_y * freq_y) <= cutoff
    cosine = jnp.cos(phase)
    sine = jnp.sin(phase)
    w_real = weight_ref[0:1, :]
    w_imag = weight_ref[1:2, :]
    c_real = jnp.where(inside, w_real * cosine + w_imag * sine, 0.0)
    c_imag = jnp.where(inside, w_imag * cosine - w_real * sine, 0.0)
    is_real = lax.broadcasted_iota(jnp.int32, (rows, 1), 0) % unit < unit // 2
    first = jnp.where(is_real, c_real, c_imag).astype(jnp.bfloat16)
    second = jnp.where(is_real, -c_imag, c_real).astype(jnp.bfloat16)
    step = GRID // TILE_SIDE
    window = shift_x // step * TILE_SIDE + shift_y // step
    place_of = lax.broadcasted_iota(jnp.int32, (1, width), 1)
    chosen = window == place_of % tile_count
    spread = lax.broadcasted_iota(jnp.int32, (local, width), 1) // tile_count
    spread = (spread == lax.broadcasted_iota(jnp.int32, (local, width), 0)).astype(jnp.float32).astype(jnp.bfloat16)
    for at, part in ((0, first), (width, second)):
        full = jnp.dot(part, spread, preferred_element_type=jnp.float32)
        left_ref[:, at : at + width] = jnp.where(chosen, full, 0.0).astype(jnp.bfloat16)

    if other != strides:
        for at, old in moves:
            mixed_left[at : at + unit, :] = left_ref[old : old + unit, :]

    def left_of(c):
        return left_ref if order(c) == strides else mixed_left

    def res_of(c):
        return res_ref if order(c) == strides else mixed_res

    narrow = min(MATMUL_COLUMNS, wide)

    def multiply(c):
        def tile(i, carry):
            at = pl.ds(pl.multiple_of(c * wide + i * narrow, narrow), narrow)
            acc[:, at] = jnp.dot(left_of(c)[...], s_vmem[:, at], preferred_element_type=jnp.float32)
            return carry

        lax.fori_loop(0, wide // narrow, tile, 0)

    def scatter_rows(c, k):
        size = rows // 2 ** (k + 1)
        base = place(me, order(c), unit, k)
        bit = (me // order(c)[k]) % 2
        keep = pl.ds(pl.multiple_of(base + bit * size, size), size)
        give = pl.ds(pl.multiple_of(base + (1 - bit) * size, size), size)
        slot = pl.ds(rows - 2 * size, size)
        return keep, give, slot

    def start_scatter(c, k):
        _, give, slot = scatter_rows(c, k)
        sbuf[slot, columns(c)] = acc[give, columns(c)].astype(jnp.bfloat16)
        return send(
            sbuf.at[slot, columns(c)],
            rbuf.at[slot, columns(c)],
            send_sem.at[c, k],
            recv_sem.at[c, k],
            partner(order(c)[k]),
        )

    def end_scatter(c, k):
        keep, _, slot = scatter_rows(c, k)
        acc[keep, columns(c)] += rbuf[slot, columns(c)].astype(jnp.float32)

    def residual(c):
        own = mine(levels, order(c))
        scale = jnp.exp2(par_ref[:, 3:4].astype(jnp.float32))
        goal = target_ref[:, columns(c)].astype(jnp.float32) * scale
        res_of(c)[own, columns(c)] = (acc[own, columns(c)] - goal).astype(jnp.bfloat16)

    def start_gather(c, k):
        held = res_of(c).at[mine(k + 1, order(c)), columns(c)]
        at = 2 * levels - 1 - k
        return send(held, held, send_sem.at[c, at], recv_sem.at[c, at], partner(order(c)[k]))

    def slots(c):
        hops = order(c) + order(c)[::-1]
        taken = [0]
        for stride in hops:
            taken.append(taken[-1] + (GAP_NEAR if stride == 1 else GAP_FAR))
        return taken

    flight = {}
    for time in range(CHUNKS + slots(0)[-1]):
        for c in range(CHUNKS):
            if time - c not in slots(c):
                continue
            at = slots(c).index(time - c)
            if at == 0:
                loads[c].wait()
                multiply(c)
            else:
                flight[c].wait_recv()
                if at <= levels:
                    end_scatter(c, at - 1)
            if at < levels:
                flight[c] = start_scatter(c, at)
            elif at < 2 * levels:
                if at == levels:
                    residual(c)
                flight[c] = start_gather(c, 2 * levels - 1 - at)
    for c in range(CHUNKS):
        if order(c) != strides:
            for at, old in moves:
                res_ref[old : old + unit, columns(c)] = mixed_res[at : at + unit, columns(c)]
    for copy in sent:
        copy.wait_send()


def grad_kernel(left_ref, res_ref, out_ref):
    dims = (((0,), (0,)), ((), ()))
    out_ref[...] = lax.dot_general(left_ref[...], res_ref[...], dims, preferred_element_type=jnp.float32).astype(
        out_ref.dtype
    )


def grad_by_columns(left_ref, res_ref, out_ref):
    dims = (((0,), (0,)), ((), ()))
    out_ref[...] = lax.dot_general(left_ref[...], res_ref[0], dims, preferred_element_type=jnp.float32).astype(
        out_ref.dtype
    )


def grid_body(n, s_matrix, beam_weight, probe_shift, probe_cutoff, target, target_exp):
    _, local, tile_count, pixels = s_matrix.shape
    probes = probe_shift.shape[0]
    unit = 2 * probes
    rows = n * unit
    block = rows // 8
    width = local * tile_count
    chunks = len(KINDS)
    wide = pixels // chunks
    pars = jnp.concatenate([probe_shift, probe_cutoff[:, None], target_exp[:, None]], axis=1)
    pars = jnp.pad(jnp.concatenate([pars, pars], axis=0), ((0, 0), (0, 124)))
    vmem = pl.BlockSpec(memory_space=pltpu.VMEM)
    res, left = pl.pallas_call(
        functools.partial(grid_kernel, n, local, tile_count, pixels),
        out_shape=(
            jax.ShapeDtypeStruct((chunks, 2, 2, 2, block, wide), jnp.bfloat16),
            jax.ShapeDtypeStruct((rows, 2 * width), jnp.bfloat16),
        ),
        in_specs=[vmem, vmem, vmem, pl.BlockSpec(memory_space=pl.ANY)],
        out_specs=(vmem, vmem),
        scratch_shapes=[
            pltpu.VMEM((rows, 128), jnp.int32),
            pltpu.VMEM((2 * width, pixels), jnp.bfloat16),
            pltpu.VMEM((chunks, 2, 2, 2, block, wide), jnp.float32),
            pltpu.VMEM((chunks, 2, 2, 2, block, wide), jnp.bfloat16),
            pltpu.VMEM((chunks, 2, 2, block, wide), jnp.bfloat16),
            pltpu.VMEM((chunks, 2, block, wide), jnp.bfloat16),
            pltpu.VMEM((chunks, 2, 2, block, wide), jnp.bfloat16),
            pltpu.VMEM((chunks, 2, block, wide), jnp.bfloat16),
            pltpu.SemaphoreType.DMA((n - 1,)),
            pltpu.SemaphoreType.DMA((n - 1,)),
            pltpu.SemaphoreType.DMA((chunks,)),
            pltpu.SemaphoreType.DMA((chunks, 12)),
            pltpu.SemaphoreType.DMA((chunks, len(NAMES))),
        ],
        compiler_params=pltpu.CompilerParams(
            collective_id=0, has_side_effects=True, vmem_limit_bytes=60 * 2**20
        ),
    )(pars, beam_weight, target.reshape(unit, pixels), s_matrix.reshape(2 * width, pixels))
    grad = pl.pallas_call(
        grad_by_columns,
        grid=(chunks,),
        out_shape=jax.ShapeDtypeStruct((2 * width, pixels), jnp.bfloat16),
        in_specs=[
            pl.BlockSpec((rows, 2 * width), lambda i: (0, 0)),
            pl.BlockSpec((1, rows, wide), lambda i: (i, 0, 0)),
        ],
        out_specs=pl.BlockSpec((2 * width, wide), lambda i: (0, i)),
        compiler_params=pltpu.CompilerParams(vmem_limit_bytes=60 * 2**20),
    )(left, res.reshape(chunks, rows, wide))
    return grad.reshape(2, local, tile_count, pixels)


def body(n, s_matrix, beam_weight, probe_shift, probe_cutoff, target, target_exp):
    if n == 16:
        return grid_body(n, s_matrix, beam_weight, probe_shift, probe_cutoff, target, target_exp)
    _, local, tile_count, pixels = s_matrix.shape
    probes = probe_shift.shape[0]
    strides, other = orders(n)
    levels = len(strides)
    unit = 2 * probes
    rows = n * unit
    width = local * tile_count
    pars = jnp.concatenate([probe_shift, probe_cutoff[:, None], target_exp[:, None]], axis=1)
    pars = jnp.pad(jnp.concatenate([pars, pars], axis=0), ((0, 0), (0, 124)))
    vmem = pl.BlockSpec(memory_space=pltpu.VMEM)
    res, left = pl.pallas_call(
        functools.partial(wave_kernel, n, local, tile_count, pixels, strides, other),
        out_shape=(
            jax.ShapeDtypeStruct((rows, pixels), jnp.bfloat16),
            jax.ShapeDtypeStruct((rows, 2 * width), jnp.bfloat16),
        ),
        in_specs=[vmem, vmem, vmem, pl.BlockSpec(memory_space=pl.ANY)],
        out_specs=(vmem, vmem),
        scratch_shapes=[
            pltpu.VMEM((rows, 128), jnp.int32),
            pltpu.VMEM((2 * width, pixels), jnp.bfloat16),
            pltpu.VMEM((rows, pixels), jnp.float32),
            pltpu.VMEM((rows, pixels), jnp.bfloat16),
            pltpu.VMEM((rows, pixels), jnp.bfloat16),
            pltpu.VMEM((rows, 2 * width), jnp.bfloat16),
            pltpu.VMEM((rows, pixels), jnp.bfloat16),
            pltpu.SemaphoreType.DMA((n - 1,)),
            pltpu.SemaphoreType.DMA((n - 1,)),
            pltpu.SemaphoreType.DMA((CHUNKS,)),
            pltpu.SemaphoreType.DMA((CHUNKS, 2 * levels)),
            pltpu.SemaphoreType.DMA((CHUNKS, 2 * levels)),
        ],
        compiler_params=pltpu.CompilerParams(
            collective_id=0, has_side_effects=True, vmem_limit_bytes=60 * 2**20
        ),
    )(pars, beam_weight, target.reshape(unit, pixels), s_matrix.reshape(2 * width, pixels))
    tall = min(512, width)
    grad = pl.pallas_call(
        grad_kernel,
        grid=(2 * width // tall,),
        out_shape=jax.ShapeDtypeStruct((2 * width, pixels), jnp.bfloat16),
        in_specs=[
            pl.BlockSpec((rows, tall), lambda i: (0, i)),
            pl.BlockSpec((rows, pixels), lambda i: (0, 0)),
        ],
        out_specs=pl.BlockSpec((tall, pixels), lambda i: (i, 0)),
        compiler_params=pltpu.CompilerParams(vmem_limit_bytes=60 * 2**20),
    )(left, res)
    return grad.reshape(2, local, tile_count, pixels)


def solution(mesh):
    return jax.shard_map(
        functools.partial(body, mesh.shape["beam"]),
        mesh=mesh,
        in_specs=(
            P(None, ("grp", "beam"), None, None),
            P(None, ("grp", "beam")),
            P(("grp", "beam"), None),
            P(("grp", "beam")),
            P(None, ("grp", "beam"), None),
            P(("grp", "beam")),
        ),
        out_specs=P(None, ("grp", "beam"), None, None),
        check_vma=False,
    )
```

```python
import functools
import math

import jax
import jax.numpy as jnp
from jax import lax
from jax.experimental import pallas as pl
from jax.experimental.pallas import tpu as pltpu
from jax.sharding import PartitionSpec as P

SIDE = 32
GRID = 192
TILE_SIDE = 4
TWO_PI = 2.0 * math.pi
CHUNKS = 8
SWAP = True
GAP_NEAR = 2
GAP_FAR = 4
MATMUL_COLUMNS = 512


KINDS = ("YY",) * 8
LINK_RATE = 46.5e3
CORE_RATE = 250e3
LINK_LAG = 1.66
CORE_LAG = 0.9
PRODUCT_US = 5.5
ADD_US = 0.3
GRADIENT_US = 10.0
TURN_US = 0.5
NAMES = ("r1", "r2", "r3f", "r3n", "r4", "ga", "gb", "gn1", "gn2", "gf1", "gf2", "ac")


def steps_of(inner, kind, more):
    sums, spread = kind
    steps = [("M", (), (("c", "r1", 4),), 0, ())]
    if spread == "Y":
        first = (("m", "gf1", 1), ("o", "gn1", 1), ("y", "ga", 1))
    else:
        first = (("y", "ga", 1), ("m", "gf1", 1), ("o", "gn1", 1))
    edge_sums = (("t", "r3f", 1), ("t", "r3n", 1)) if sums == "Y" else (("t", "r3f", 2), ("t", "r3n", 2))
    if sums == "Y":
        steps.append(("C", ("r1",), (("y", "r2", 2),), 4, ("M",)))
        if inner:
            steps.append(("Y", ("r2",), (), 2, ("C",)))
            steps.append(("F", ("r3f",), (("m", "r4", 1),), 1, ("Y",)))
            steps.append(("N", ("r3n", "r4"), first, 1, ("F",)))
        else:
            steps.append(("Y", ("r2",), edge_sums, 2, ("C",)))
        last = "N"
    else:
        if inner:
            steps.append(("C", ("r1",), (), 4, ("M",)))
            steps.append(("F", ("r3f",), (("m", "r4", 2),), 2, ("C",)))
            steps.append(("N", ("r3n", "r4"), (("y", "r2", 1),), 2, ("F",)))
            steps.append(("Y", ("r2",), first, 1, ("N",)))
        else:
            steps.append(("C", ("r1",), edge_sums, 4, ("M",)))
        last = "Y"
    if spread == "Y":
        if inner:
            steps.append(("G1", ("gf1",), (("o", "gf1", 1), ("y", "gb", 1)), 0, ()))
            steps.append(("A", ("ga", "gb"), (("c", "ac", 4),), 0, (last, "G1")))
        else:
            steps.append(("G1", ("gn1",), (("y", "ga", 1),), 0, ()))
            steps.append(("G2", ("gf1",), (("y", "gb", 1),), 0, ()))
            steps.append(("A", ("ga", "gb"), (("c", "ac", 4),), 0, ("G1", "G2")))
    elif inner:
        steps.append(("H", ("ga",), (("m", "gf2", 1), ("o", "gn2", 1)), 0, ()))
        steps.append(("G1", ("gf1",), (("o", "gf1", 1),), 0, ()))
        steps.append(("A", ("gf2",), (("o", "gf2", 1), ("c", "ac", 4)), 0, (last, "H", "G1")))
    else:
        steps.append(("A", ("gn1", "gn2", "gf1", "gf2"), (("c", "ac", 4),), 0, ()))
    steps.append(("E", ("ac",), (), 0, ()))
    if more:
        steps.append(("P0", (), (), 0, ("E",)))
        steps.append(("P1", (), (), 0, ("P0",)))
    else:
        steps.append(("T0", (), (), 0, ("M",)))
        steps.append(("T1", (), (), 0, ("T0",)))
    return steps


def schedule(block_bytes):
    chunks = len(KINDS)
    waiting = [[(k, step) for k in range(chunks) for step in steps_of(inner, KINDS[k], k < chunks - 1)] for inner in (False, True)]
    arrived, done = ({}, {}), ({}, {})
    free, links = [0.0, 0.0], {}
    order = ([], [])
    while waiting[0] or waiting[1]:
        best = None
        for role in (0, 1):
            for k, step in waiting[role]:
                name, needs, _, _, after = step
                if name == "M" and k > 0 and (k - 1, "M") not in done[role]:
                    continue
                if name == "P0" and (chunks - 1, "T1") not in done[role]:
                    continue
                if any((k, x) not in arrived[role] for x in needs) or any((k, x) not in done[role] for x in after):
                    continue
                ready = max([free[role]] + [arrived[role][k, x] for x in needs])
                rank = (ready, name[0] in "MPT", name[0] in "PT", k, role, name)
                if best is None or rank < best[0]:
                    best = (rank, role, k, step)
        (ready, *_), role, k, step = best
        name, _, sends, blocks, _ = step
        cost = {"M": PRODUCT_US / chunks, "P": GRADIENT_US / 2 / chunks, "T": TURN_US}
        end = ready + cost.get(name[0], 0.02 + ADD_US * blocks / chunks)
        free[role] = end
        done[role][k, name] = end
        waiting[role].remove((k, step))
        order[role].append((k, name))
        for link, message, count in sends:
            rate, lag = (CORE_RATE, CORE_LAG) if link == "c" else (LINK_RATE, LINK_LAG)
            sent = max(end, links.get((role, link), 0.0)) + count * block_bytes / rate
            links[role, link] = sent
            arrived[{"t": 1, "o": 0}.get(link, role)][k, message] = sent + lag
    return order


def grid_kernel(
    n, local, tile_count, pixels,
    shift_ref, cutoff_ref, exp_ref, weight_ref, target_hbm, s_ref,
    grad_ref, res_ref, turned_ref,
    raw, par_ref, target_ref, parts, left_ref, pars, acc, sbuf, r1, r2, r3, r4,
    par_send, par_recv, s_sem, send_sem, recv_sem,
):
    me = lax.axis_index("beam")
    unit = par_ref.shape[0]
    rows = n * unit
    width = local * tile_count
    s_vmem = grad_ref
    chunks = len(KINDS)
    wide = pixels // chunks
    block = rows // 8
    core, across, line = me % 2, me // 2 % 2, me // 4
    side = line // 2
    far = 1 - side
    inward = (1 - 2 * side) * 4
    peers = {
        "c": me + 1 - 2 * core,
        "y": me + 2 - 4 * across,
        "t": me + inward,
        "m": me + inward,
        "o": me - inward,
    }

    def columns(k):
        return pl.ds(k * wide, wide)

    loads = []
    for k in range(chunks):
        load = pltpu.make_async_copy(s_ref.at[:, columns(k)], s_vmem.at[:, columns(k)], s_sem.at[k])
        loads.append(load)
    target_load = pltpu.make_async_copy(target_hbm, target_ref, s_sem.at[chunks])
    barrier = pltpu.get_barrier_semaphore()
    for ahead in range(1, n):
        pl.semaphore_signal(
            barrier, inc=1, device_id={"beam": lax.rem(me + ahead, n)}, device_id_type=pl.DeviceIdType.MESH
        )
    target_load.start()
    for load in loads:
        load.start()
    probes = unit // 2
    raw[...] = jnp.zeros_like(raw)
    raw[0:2, 0:probes] = shift_ref[...]
    raw[2:3, 0:probes] = cutoff_ref[...]
    raw[3:4, 0:probes] = exp_ref[...]
    table = raw[...].T[0:probes, :]
    par_ref[...] = jnp.zeros_like(par_ref)
    par_ref[0:probes, 0:8] = table
    par_ref[probes:unit, 0:8] = table
    pl.semaphore_wait(barrier, n - 1)

    def remote(source, target, send_semaphore, recv_semaphore, peer):
        return pltpu.make_async_remote_copy(
            src_ref=source,
            dst_ref=target,
            send_sem=send_semaphore,
            recv_sem=recv_semaphore,
            device_id={"beam": peer},
            device_id_type=pl.DeviceIdType.MESH,
        )

    mine = pl.ds(pl.multiple_of(me * unit, unit), unit)
    pars[mine, :] = par_ref[...]
    asked = [
        remote(par_ref, pars.at[mine, :], par_send.at[ahead - 1], par_recv.at[ahead - 1], lax.rem(me + ahead, n))
        for ahead in range(1, n)
    ]
    for copy in asked:
        copy.start()
    for copy in asked:
        copy.wait_recv()

    half = SIDE // 2
    beam = me * local + lax.broadcasted_iota(jnp.int32, (1, local), 1)
    freq_x = beam % SIDE - half
    freq_y = beam // SIDE - half
    shift_x = pars[:, 0:1]
    shift_y = pars[:, 1:2]
    cutoff = pars[:, 2:3]
    ramp = (freq_x * shift_x + freq_y * shift_y) % GRID
    phase = ramp.astype(jnp.float32) * (TWO_PI / GRID)
    inside = (freq_x * freq_x + freq_y * freq_y) <= cutoff
    cosine = jnp.cos(phase)
    sine = jnp.sin(phase)
    w_real = weight_ref[0:1, :]
    w_imag = weight_ref[1:2, :]
    c_real = jnp.where(inside, w_real * cosine + w_imag * sine, 0.0)
    c_imag = jnp.where(inside, w_imag * cosine - w_real * sine, 0.0)
    is_real = lax.broadcasted_iota(jnp.int32, (rows, 1), 0) % unit < unit // 2
    first = jnp.where(is_real, c_real, c_imag).astype(jnp.bfloat16)
    second = jnp.where(is_real, -c_imag, c_real).astype(jnp.bfloat16)
    step = GRID // TILE_SIDE
    window = shift_x // step * TILE_SIDE + shift_y // step
    place_of = lax.broadcasted_iota(jnp.int32, (1, width), 1)
    chosen = window == place_of % tile_count
    spread = lax.broadcasted_iota(jnp.int32, (local, width), 1) // tile_count
    spread = (spread == lax.broadcasted_iota(jnp.int32, (local, width), 0)).astype(jnp.float32).astype(jnp.bfloat16)
    for at, part in ((0, first), (width, second)):
        full = jnp.dot(part, spread, preferred_element_type=jnp.float32)
        left_ref[:, at : at + width] = jnp.where(chosen, full, 0.0).astype(jnp.bfloat16)
    parts[0] = first
    parts[1] = second
    target_load.wait()

    def turn(part):
        window_row = jnp.broadcast_to(window.astype(jnp.float32), (rows, 128)).T[0:1, :]
        tile = lax.broadcasted_iota(jnp.int32, (width, 1), 0) % tile_count
        beams = lax.broadcasted_iota(jnp.int32, (width, local), 0) // tile_count
        beams = (beams == lax.broadcasted_iota(jnp.int32, (width, local), 1)).astype(jnp.float32).astype(jnp.bfloat16)
        full = lax.dot_general(beams, parts[part], (((1,), (1,)), ((), ())), preferred_element_type=jnp.float32)
        chosen_row = tile.astype(jnp.float32) == window_row
        turned_ref[part * width : (part + 1) * width, :] = jnp.where(chosen_row, full, 0.0).astype(jnp.bfloat16)

    own = (me * unit // block // 4, me * unit // block // 2 % 2, me * unit // block % 2)
    own_rows = pl.ds(pl.multiple_of(me * unit % block, unit), unit)

    def run(inner, steps):
        sent = []

        def send(k, link, message, source, target):
            copy = remote(
                source, target, send_sem.at[k, len([1 for other, _ in sent if other == k])],
                recv_sem.at[k, NAMES.index(message)], peers[link],
            )
            copy.start()
            sent.append((k, copy))

        def got(k, message, view):
            remote(view, view, send_sem.at[k, 0], recv_sem.at[k, NAMES.index(message)], peers["c"]).wait_recv()

        def low(x):
            return x.astype(jnp.bfloat16)

        def spread_first(k):
            held = res_ref.at[k, core, across, side]
            if KINDS[k][1] == "Y":
                send(k, "m", "gf1", held, held)
                send(k, "o", "gn1", held, held)
                send(k, "y", "ga", held, held)
            else:
                send(k, "y", "ga", held, held)
                send(k, "m", "gf1", held, held)
                send(k, "o", "gn1", held, held)

        def take(k, name):
            by_y = KINDS[k][0] == "Y"
            at = (k, core, across)
            here = (k, core, across, side)
            if name == "M":
                loads[k].wait()
                product = jnp.dot(left_ref[...], s_vmem[:, columns(k)], preferred_element_type=jnp.float32)
                acc[k] = product.reshape(2, 2, 2, block, wide)
                goal = target_ref[:, columns(k)].astype(jnp.float32) * jnp.exp2(par_ref[:, 3:4].astype(jnp.float32))
                acc[(k, *own, own_rows)] = acc[(k, *own, own_rows)] - goal
                sbuf[k, 1 - core] = low(acc[k, 1 - core])
                send(k, "c", "r1", sbuf.at[k, 1 - core], r1.at[k])
            elif name == "C":
                got(k, "r1", r1.at[k])
                if by_y:
                    sbuf[k, core, 1 - across] = low(acc[k, core, 1 - across] + r1[k, 1 - across].astype(jnp.float32))
                    send(k, "y", "r2", sbuf.at[k, core, 1 - across], r2.at[k])
                    acc[at] = acc[at] + r1[k, across].astype(jnp.float32)
                elif inner:
                    acc[k, core] = acc[k, core] + r1[k].astype(jnp.float32)
                else:
                    for at_side, message, slot in ((far, "r3f", 0), (side, "r3n", 1)):
                        total = acc[k, core, :, at_side] + r1[k, :, at_side].astype(jnp.float32)
                        sbuf[k, core, :, at_side] = low(total)
                        send(k, "t", message, sbuf.at[k, core, :, at_side], r3.at[k, slot])
            elif name == "Y":
                if by_y:
                    got(k, "r2", r2.at[k])
                    total = acc[at] + r2[k].astype(jnp.float32)
                    if inner:
                        acc[at] = total
                    else:
                        sbuf[at] = low(total)
                        send(k, "t", "r3f", sbuf.at[(*at, far)], r3.at[k, 0, 0])
                        send(k, "t", "r3n", sbuf.at[(*at, side)], r3.at[k, 1, 0])
                else:
                    got(k, "r2", r2.at[k, 0])
                    res_ref[here] = low(acc[here] + r2[k, 0].astype(jnp.float32))
                    spread_first(k)
            elif name == "F":
                if by_y:
                    got(k, "r3f", r3.at[k, 0, 0])
                    sbuf[(*at, far)] = low(acc[(*at, far)] + r3[k, 0, 0].astype(jnp.float32))
                    send(k, "m", "r4", sbuf.at[(*at, far)], r4.at[k, 0])
                else:
                    got(k, "r3f", r3.at[k, 0])
                    sbuf[k, core, :, far] = low(acc[k, core, :, far] + r3[k, 0].astype(jnp.float32))
                    send(k, "m", "r4", sbuf.at[k, core, :, far], r4.at[k])
            elif name == "N":
                if by_y:
                    got(k, "r3n", r3.at[k, 1, 0])
                    got(k, "r4", r4.at[k, 0])
                    total = acc[here] + r3[k, 1, 0].astype(jnp.float32) + r4[k, 0].astype(jnp.float32)
                    res_ref[here] = low(total)
                    spread_first(k)
                else:
                    got(k, "r3n", r3.at[k, 1])
                    got(k, "r4", r4.at[k])
                    there = (k, core, 1 - across, side)
                    total = acc[there] + r3[k, 1, 1 - across].astype(jnp.float32) + r4[k, 1 - across].astype(jnp.float32)
                    sbuf[there] = low(total)
                    send(k, "y", "r2", sbuf.at[there], r2.at[k, 0])
                    acc[here] = acc[here] + r3[k, 1, across].astype(jnp.float32) + r4[k, across].astype(jnp.float32)
            elif name == "A":
                if KINDS[k][1] == "Y":
                    got(k, "ga", res_ref.at[here])
                    got(k, "gb", res_ref.at[here])
                elif inner:
                    got(k, "gf2", res_ref.at[here])
                    held = res_ref.at[k, core, 1 - across, far]
                    send(k, "o", "gf2", held, held)
                else:
                    for message in ("gn1", "gn2", "gf1", "gf2"):
                        got(k, message, res_ref.at[here])
                send(k, "c", "ac", res_ref.at[k, core], res_ref.at[k, core])
            elif name == "H":
                got(k, "ga", res_ref.at[here])
                held = res_ref.at[k, core, 1 - across, side]
                send(k, "m", "gf2", held, held)
                send(k, "o", "gn2", held, held)
            elif name == "G1":
                if inner:
                    got(k, "gf1", res_ref.at[here])
                    held = res_ref.at[(*at, far)]
                    send(k, "o", "gf1", held, held)
                    if KINDS[k][1] == "Y":
                        send(k, "y", "gb", held, held)
                else:
                    got(k, "gn1", res_ref.at[here])
                    held = res_ref.at[here]
                    send(k, "y", "ga", held, held)
            elif name == "G2":
                got(k, "gf1", res_ref.at[here])
                held = res_ref.at[(*at, far)]
                send(k, "y", "gb", held, held)
            elif name == "E":
                got(k, "ac", res_ref.at[k, 1 - core])
            elif name in ("P0", "P1"):
                half_rows = pl.ds(int(name[1]) * width, width)
                product = jnp.dot(
                    turned_ref[half_rows, :], res_ref[k].reshape(rows, wide), preferred_element_type=jnp.float32
                )
                grad_ref[half_rows, columns(k)] = low(product)
            elif name in ("T0", "T1"):
                turn(int(name[1]))

        for k, name in steps:
            take(k, name)
        for _, copy in sent:
            copy.wait_send()

    edge_steps, inner_steps = schedule(block * wide * 2)
    middle = (line == 1) | (line == 2)

    @pl.when(middle)
    def _():
        run(True, inner_steps)

    @pl.when(jnp.logical_not(middle))
    def _():
        run(False, edge_steps)

    for copy in asked:
        copy.wait_send()


def stage_strides(n):
    return [2**k for k in range(n.bit_length() - 1)]


def orders(n):
    strides = stage_strides(n)
    other = list(strides)
    if SWAP and len(other) > 2:
        other[1], other[2] = other[2], other[1]
    return strides, other


def place(me, strides, unit, upto):
    levels = len(strides)
    base = 0
    for k in range(upto):
        base = base + (me // strides[k]) % 2 * (unit * 2 ** (levels - 1 - k))
    return base


def wave_kernel(
    n, local, tile_count, pixels, strides, other,
    par_ref, weight_ref, target_ref, s_ref,
    res_ref, left_ref,
    pars, s_vmem, acc, sbuf, rbuf, mixed_left, mixed_res,
    par_send, par_recv, s_sem, send_sem, recv_sem,
):
    levels = len(strides)
    me = lax.axis_index("beam")
    unit = par_ref.shape[0]
    rows = n * unit
    width = local * tile_count
    wide = pixels // CHUNKS

    def order(c):
        return other if c % 2 else strides

    moves = [(place(i, other, unit, levels), place(i, strides, unit, levels)) for i in range(n)]

    def partner(stride):
        return me + (1 - 2 * ((me // stride) % 2)) * stride

    def columns(c):
        return pl.ds(c * wide, wide)

    loads = []
    for c in range(CHUNKS):
        load = pltpu.make_async_copy(s_ref.at[:, columns(c)], s_vmem.at[:, columns(c)], s_sem.at[c])
        load.start()
        loads.append(load)

    barrier = pltpu.get_barrier_semaphore()
    for ahead in range(1, n):
        pl.semaphore_signal(
            barrier, inc=1, device_id={"beam": lax.rem(me + ahead, n)}, device_id_type=pl.DeviceIdType.MESH
        )
    pl.semaphore_wait(barrier, n - 1)

    sent = []

    def send(source, target, send_semaphore, recv_semaphore, peer):
        copy = pltpu.make_async_remote_copy(
            src_ref=source,
            dst_ref=target,
            send_sem=send_semaphore,
            recv_sem=recv_semaphore,
            device_id={"beam": peer},
            device_id_type=pl.DeviceIdType.MESH,
        )
        copy.start()
        sent.append(copy)
        return copy

    def mine(k, steps=strides):
        size = unit * 2 ** (levels - k)
        return pl.ds(pl.multiple_of(place(me, steps, unit, k), size), size)

    pars[mine(levels), :] = par_ref[...]
    asked = [
        send(par_ref, pars.at[mine(levels), :], par_send.at[ahead - 1], par_recv.at[ahead - 1], lax.rem(me + ahead, n))
        for ahead in range(1, n)
    ]
    for copy in asked:
        copy.wait_recv()

    half = SIDE // 2
    beam = me * local + lax.broadcasted_iota(jnp.int32, (1, local), 1)
    freq_x = beam % SIDE - half
    freq_y = beam // SIDE - half
    shift_x = pars[:, 0:1]
    shift_y = pars[:, 1:2]
    cutoff = pars[:, 2:3]
    ramp = (freq_x * shift_x + freq_y * shift_y) % GRID
    phase = ramp.astype(jnp.float32) * (TWO_PI / GRID)
    inside = (freq_x * freq_x + freq_y * freq_y) <= cutoff
    cosine = jnp.cos(phase)
    sine = jnp.sin(phase)
    w_real = weight_ref[0:1, :]
    w_imag = weight_ref[1:2, :]
    c_real = jnp.where(inside, w_real * cosine + w_imag * sine, 0.0)
    c_imag = jnp.where(inside, w_imag * cosine - w_real * sine, 0.0)
    is_real = lax.broadcasted_iota(jnp.int32, (rows, 1), 0) % unit < unit // 2
    first = jnp.where(is_real, c_real, c_imag).astype(jnp.bfloat16)
    second = jnp.where(is_real, -c_imag, c_real).astype(jnp.bfloat16)
    step = GRID // TILE_SIDE
    window = shift_x // step * TILE_SIDE + shift_y // step
    place_of = lax.broadcasted_iota(jnp.int32, (1, width), 1)
    chosen = window == place_of % tile_count
    spread = lax.broadcasted_iota(jnp.int32, (local, width), 1) // tile_count
    spread = (spread == lax.broadcasted_iota(jnp.int32, (local, width), 0)).astype(jnp.float32).astype(jnp.bfloat16)
    for at, part in ((0, first), (width, second)):
        full = jnp.dot(part, spread, preferred_element_type=jnp.float32)
        left_ref[:, at : at + width] = jnp.where(chosen, full, 0.0).astype(jnp.bfloat16)

    if other != strides:
        for at, old in moves:
            mixed_left[at : at + unit, :] = left_ref[old : old + unit, :]

    def left_of(c):
        return left_ref if order(c) == strides else mixed_left

    def res_of(c):
        return res_ref if order(c) == strides else mixed_res

    narrow = min(MATMUL_COLUMNS, wide)

    def multiply(c):
        def tile(i, carry):
            at = pl.ds(pl.multiple_of(c * wide + i * narrow, narrow), narrow)
            acc[:, at] = jnp.dot(left_of(c)[...], s_vmem[:, at], preferred_element_type=jnp.float32)
            return carry

        lax.fori_loop(0, wide // narrow, tile, 0)

    def scatter_rows(c, k):
        size = rows // 2 ** (k + 1)
        base = place(me, order(c), unit, k)
        bit = (me // order(c)[k]) % 2
        keep = pl.ds(pl.multiple_of(base + bit * size, size), size)
        give = pl.ds(pl.multiple_of(base + (1 - bit) * size, size), size)
        slot = pl.ds(rows - 2 * size, size)
        return keep, give, slot

    def start_scatter(c, k):
        _, give, slot = scatter_rows(c, k)
        sbuf[slot, columns(c)] = acc[give, columns(c)].astype(jnp.bfloat16)
        return send(
            sbuf.at[slot, columns(c)],
            rbuf.at[slot, columns(c)],
            send_sem.at[c, k],
            recv_sem.at[c, k],
            partner(order(c)[k]),
        )

    def end_scatter(c, k):
        keep, _, slot = scatter_rows(c, k)
        acc[keep, columns(c)] += rbuf[slot, columns(c)].astype(jnp.float32)

    def residual(c):
        own = mine(levels, order(c))
        scale = jnp.exp2(par_ref[:, 3:4].astype(jnp.float32))
        goal = target_ref[:, columns(c)].astype(jnp.float32) * scale
        res_of(c)[own, columns(c)] = (acc[own, columns(c)] - goal).astype(jnp.bfloat16)

    def start_gather(c, k):
        held = res_of(c).at[mine(k + 1, order(c)), columns(c)]
        at = 2 * levels - 1 - k
        return send(held, held, send_sem.at[c, at], recv_sem.at[c, at], partner(order(c)[k]))

    def slots(c):
        hops = order(c) + order(c)[::-1]
        taken = [0]
        for stride in hops:
            taken.append(taken[-1] + (GAP_NEAR if stride == 1 else GAP_FAR))
        return taken

    flight = {}
    for time in range(CHUNKS + slots(0)[-1]):
        for c in range(CHUNKS):
            if time - c not in slots(c):
                continue
            at = slots(c).index(time - c)
            if at == 0:
                loads[c].wait()
                multiply(c)
            else:
                flight[c].wait_recv()
                if at <= levels:
                    end_scatter(c, at - 1)
            if at < levels:
                flight[c] = start_scatter(c, at)
            elif at < 2 * levels:
                if at == levels:
                    residual(c)
                flight[c] = start_gather(c, 2 * levels - 1 - at)
    for c in range(CHUNKS):
        if order(c) != strides:
            for at, old in moves:
                res_ref[old : old + unit, columns(c)] = mixed_res[at : at + unit, columns(c)]
    for copy in sent:
        copy.wait_send()


def grad_kernel(left_ref, res_ref, out_ref):
    dims = (((0,), (0,)), ((), ()))
    out_ref[...] = lax.dot_general(left_ref[...], res_ref[...], dims, preferred_element_type=jnp.float32).astype(
        out_ref.dtype
    )


def finish_kernel(done_ref, turned_ref, res_ref, out_ref, last, sem):
    height = turned_ref.shape[0]
    chunks, _, wide = res_ref.shape
    ready = out_ref.shape[1] - wide
    tall = height // 4
    copies = []
    for i in range(4):
        at = pl.ds(i * tall, tall)
        copies.append(pltpu.make_async_copy(done_ref.at[at, pl.ds(0, ready)], out_ref.at[at, pl.ds(0, ready)], sem.at[i]))
        copies[-1].start()
    for i in range(4):
        at = pl.ds(i * tall, tall)
        last[at, :] = jnp.dot(turned_ref[at, :], res_ref[chunks - 1], preferred_element_type=jnp.float32).astype(jnp.bfloat16)
        copies.append(pltpu.make_async_copy(last.at[at, :], out_ref.at[at, pl.ds(ready, wide)], sem.at[4 + i]))
        copies[-1].start()
    for copy in copies:
        copy.wait()


def grid_body(n, s_matrix, beam_weight, probe_shift, probe_cutoff, target, target_exp):
    _, local, tile_count, pixels = s_matrix.shape
    probes = probe_shift.shape[0]
    unit = 2 * probes
    rows = n * unit
    block = rows // 8
    width = local * tile_count
    chunks = len(KINDS)
    wide = pixels // chunks
    vmem = pl.BlockSpec(memory_space=pltpu.VMEM)
    hbm = pl.BlockSpec(memory_space=pl.ANY)
    done, res, turned = pl.pallas_call(
        functools.partial(grid_kernel, n, local, tile_count, pixels),
        out_shape=(
            pltpu.VMEM((2 * width, pixels), jnp.bfloat16),
            pltpu.VMEM((chunks, 2, 2, 2, block, wide), jnp.bfloat16),
            pltpu.VMEM((2 * width, rows), jnp.bfloat16),
        ),
        in_specs=[vmem, vmem, vmem, vmem, hbm, hbm],
        out_specs=(vmem, vmem, vmem),
        scratch_shapes=[
            pltpu.VMEM((8, 128), jnp.int32),
            pltpu.VMEM((unit, 128), jnp.int32),
            pltpu.VMEM((unit, pixels), jnp.bfloat16),
            pltpu.VMEM((2, rows, local), jnp.bfloat16),
            pltpu.VMEM((rows, 2 * width), jnp.bfloat16),
            pltpu.VMEM((rows, 128), jnp.int32),
            pltpu.VMEM((chunks, 2, 2, 2, block, wide), jnp.float32),
            pltpu.VMEM((chunks, 2, 2, 2, block, wide), jnp.bfloat16),
            pltpu.VMEM((chunks, 2, 2, block, wide), jnp.bfloat16),
            pltpu.VMEM((chunks, 2, block, wide), jnp.bfloat16),
            pltpu.VMEM((chunks, 2, 2, block, wide), jnp.bfloat16),
            pltpu.VMEM((chunks, 2, block, wide), jnp.bfloat16),
            pltpu.SemaphoreType.DMA((n - 1,)),
            pltpu.SemaphoreType.DMA((n - 1,)),
            pltpu.SemaphoreType.DMA((chunks + 1,)),
            pltpu.SemaphoreType.DMA((chunks, 12)),
            pltpu.SemaphoreType.DMA((chunks, len(NAMES))),
        ],
        compiler_params=pltpu.CompilerParams(
            collective_id=0, has_side_effects=True, vmem_limit_bytes=36 * 2**20
        ),
    )(
        probe_shift.T, probe_cutoff.reshape(1, probes), target_exp.reshape(1, probes), beam_weight,
        target.reshape(unit, pixels), s_matrix.reshape(2 * width, pixels),
    )
    grad = pl.pallas_call(
        finish_kernel,
        out_shape=jax.ShapeDtypeStruct((2 * width, pixels), jnp.bfloat16),
        in_specs=[vmem, vmem, vmem],
        out_specs=hbm,
        scratch_shapes=[pltpu.VMEM((2 * width, wide), jnp.bfloat16), pltpu.SemaphoreType.DMA((8,))],
        compiler_params=pltpu.CompilerParams(vmem_limit_bytes=8 * 2**20),
    )(done, turned, res.reshape(chunks, rows, wide))
    return grad.reshape(2, local, tile_count, pixels)


def body(n, s_matrix, beam_weight, probe_shift, probe_cutoff, target, target_exp):
    if n == 16:
        return grid_body(n, s_matrix, beam_weight, probe_shift, probe_cutoff, target, target_exp)
    _, local, tile_count, pixels = s_matrix.shape
    probes = probe_shift.shape[0]
    strides, other = orders(n)
    levels = len(strides)
    unit = 2 * probes
    rows = n * unit
    width = local * tile_count
    pars = jnp.concatenate([probe_shift, probe_cutoff[:, None], target_exp[:, None]], axis=1)
    pars = jnp.pad(jnp.concatenate([pars, pars], axis=0), ((0, 0), (0, 124)))
    vmem = pl.BlockSpec(memory_space=pltpu.VMEM)
    res, left = pl.pallas_call(
        functools.partial(wave_kernel, n, local, tile_count, pixels, strides, other),
        out_shape=(
            jax.ShapeDtypeStruct((rows, pixels), jnp.bfloat16),
            jax.ShapeDtypeStruct((rows, 2 * width), jnp.bfloat16),
        ),
        in_specs=[vmem, vmem, vmem, pl.BlockSpec(memory_space=pl.ANY)],
        out_specs=(vmem, vmem),
        scratch_shapes=[
            pltpu.VMEM((rows, 128), jnp.int32),
            pltpu.VMEM((2 * width, pixels), jnp.bfloat16),
            pltpu.VMEM((rows, pixels), jnp.float32),
            pltpu.VMEM((rows, pixels), jnp.bfloat16),
            pltpu.VMEM((rows, pixels), jnp.bfloat16),
            pltpu.VMEM((rows, 2 * width), jnp.bfloat16),
            pltpu.VMEM((rows, pixels), jnp.bfloat16),
            pltpu.SemaphoreType.DMA((n - 1,)),
            pltpu.SemaphoreType.DMA((n - 1,)),
            pltpu.SemaphoreType.DMA((CHUNKS,)),
            pltpu.SemaphoreType.DMA((CHUNKS, 2 * levels)),
            pltpu.SemaphoreType.DMA((CHUNKS, 2 * levels)),
        ],
        compiler_params=pltpu.CompilerParams(
            collective_id=0, has_side_effects=True, vmem_limit_bytes=60 * 2**20
        ),
    )(pars, beam_weight, target.reshape(unit, pixels), s_matrix.reshape(2 * width, pixels))
    tall = min(512, width)
    grad = pl.pallas_call(
        grad_kernel,
        grid=(2 * width // tall,),
        out_shape=jax.ShapeDtypeStruct((2 * width, pixels), jnp.bfloat16),
        in_specs=[
            pl.BlockSpec((rows, tall), lambda i: (0, i)),
            pl.BlockSpec((rows, pixels), lambda i: (0, 0)),
        ],
        out_specs=pl.BlockSpec((tall, pixels), lambda i: (i, 0)),
        compiler_params=pltpu.CompilerParams(vmem_limit_bytes=60 * 2**20),
    )(left, res)
    return grad.reshape(2, local, tile_count, pixels)


def solution(mesh):
    return jax.shard_map(
        functools.partial(body, mesh.shape["beam"]),
        mesh=mesh,
        in_specs=(
            P(None, ("grp", "beam"), None, None),
            P(None, ("grp", "beam")),
            P(("grp", "beam"), None),
            P(("grp", "beam")),
            P(None, ("grp", "beam"), None),
            P(("grp", "beam")),
        ),
        out_specs=P(None, ("grp", "beam"), None, None),
        check_vma=False,
    )
```

```python
import functools
import math

import jax
import jax.numpy as jnp
from jax import lax
from jax.experimental import pallas as pl
from jax.experimental.pallas import tpu as pltpu
from jax.sharding import PartitionSpec as P

SIDE = 32
GRID = 192
TILE_SIDE = 4
TWO_PI = 2.0 * math.pi
CHUNKS = 8
SWAP = True
GAP_NEAR = 2
GAP_FAR = 4
MATMUL_COLUMNS = 512


KINDS = ("YY", "ZY") + ("YY",) * 6
LINK_RATE = 46.5e3
CORE_RATE = 250e3
LINK_LAG = 2.4
CORE_LAG = 1.4
PRODUCT_US = 5.5
ADD_US = 0.3
GRADIENT_US = 10.0
LATE = 3
TURN_US = 0.5
NAMES = ("r1", "r2", "r3f", "r3n", "r4", "ga", "gb", "gn1", "gn2", "gf1", "gf2", "ac")


def steps_of(inner, kind, more):
    sums, spread = kind
    steps = [("M", (), (("c", "r1", 4),), 0, ())]
    if spread == "Y":
        first = (("m", "gf1", 1), ("o", "gn1", 1), ("y", "ga", 1))
    else:
        first = (("y", "ga", 1), ("m", "gf1", 1), ("o", "gn1", 1))
    edge_sums = (("t", "r3f", 1), ("t", "r3n", 1)) if sums == "Y" else (("t", "r3f", 2), ("t", "r3n", 2))
    if sums == "Y":
        steps.append(("C", ("r1",), (("y", "r2", 2),), 4, ("M",)))
        if inner:
            steps.append(("Y", ("r2",), (), 2, ("C",)))
            steps.append(("F", ("r3f",), (("m", "r4", 1),), 1, ("Y",)))
            steps.append(("N", ("r3n", "r4"), first, 1, ("F",)))
        else:
            steps.append(("Y", ("r2",), edge_sums, 2, ("C",)))
        last = "N"
    else:
        if inner:
            steps.append(("C", ("r1",), (), 4, ("M",)))
            steps.append(("F", ("r3f",), (("m", "r4", 2),), 2, ("C",)))
            steps.append(("N", ("r3n", "r4"), (("y", "r2", 1),), 2, ("F",)))
            steps.append(("Y", ("r2",), first, 1, ("N",)))
        else:
            steps.append(("C", ("r1",), edge_sums, 4, ("M",)))
        last = "Y"
    if spread == "Y":
        if inner:
            steps.append(("G1", ("gf1",), (("o", "gf1", 1), ("y", "gb", 1)), 0, ()))
            steps.append(("A", ("ga", "gb"), (("c", "ac", 4),), 0, (last, "G1")))
        else:
            steps.append(("G1", ("gn1",), (("y", "ga", 1),), 0, ()))
            steps.append(("G2", ("gf1",), (("y", "gb", 1),), 0, ()))
            steps.append(("A", ("ga", "gb"), (("c", "ac", 4),), 0, ("G1", "G2")))
    elif inner:
        steps.append(("H", ("ga",), (("m", "gf2", 1), ("o", "gn2", 1)), 0, ()))
        steps.append(("G1", ("gf1",), (("o", "gf1", 1),), 0, ()))
        steps.append(("A", ("gf2",), (("o", "gf2", 1), ("c", "ac", 4)), 0, (last, "H", "G1")))
    else:
        steps.append(("A", ("gn1", "gn2", "gf1", "gf2"), (("c", "ac", 4),), 0, ()))
    steps.append(("E", ("ac",), (), 0, ()))
    if more > 0:
        steps.append(("P0", (), (), 0, ("E",)))
        steps.append(("P1", (), (), 0, ("P0",)))
    elif more < 0:
        steps.append(("T0", (), (), 0, ("M",)))
        steps.append(("T1", (), (), 0, ("T0",)))
    return steps


def schedule(block_bytes):
    chunks = len(KINDS)
    waiting = [[(k, step) for k in range(chunks) for step in steps_of(inner, KINDS[k], 1 - (k >= chunks - LATE) - (k == chunks - 1))] for inner in (False, True)]
    arrived, done = ({}, {}), ({}, {})
    free, links = [0.0, 0.0], {}
    order = ([], [])
    while waiting[0] or waiting[1]:
        best = None
        for role in (0, 1):
            for k, step in waiting[role]:
                name, needs, _, _, after = step
                if name == "M" and k > 0 and (k - 1, "M") not in done[role]:
                    continue
                if name == "P0" and (chunks - 1, "T1") not in done[role]:
                    continue
                if any((k, x) not in arrived[role] for x in needs) or any((k, x) not in done[role] for x in after):
                    continue
                ready = max([free[role]] + [arrived[role][k, x] for x in needs])
                rank = (ready, name[0] in "MPT", name[0] in "PT", k, role, name)
                if best is None or rank < best[0]:
                    best = (rank, role, k, step)
        (ready, *_), role, k, step = best
        name, _, sends, blocks, _ = step
        cost = {"M": PRODUCT_US / chunks, "P": GRADIENT_US / 2 / chunks, "T": TURN_US}
        end = ready + cost.get(name[0], 0.02 + ADD_US * blocks / chunks)
        free[role] = end
        done[role][k, name] = end
        waiting[role].remove((k, step))
        order[role].append((k, name))
        for link, message, count in sends:
            rate, lag = (CORE_RATE, CORE_LAG) if link == "c" else (LINK_RATE, LINK_LAG)
            sent = max(end, links.get((role, link), 0.0)) + count * block_bytes / rate
            links[role, link] = sent
            arrived[{"t": 1, "o": 0}.get(link, role)][k, message] = sent + lag
    return order


def grid_kernel(
    n, local, tile_count, pixels,
    shift_ref, cutoff_ref, exp_ref, weight_ref, target_hbm, s_ref,
    grad_ref, res_ref, turned_ref,
    raw, par_ref, scale_ref, flat, mix, target_ref, parts, left_ref, pars, acc, sbuf, r1, r2, r3, r4,
    par_send, par_recv, s_sem, send_sem, recv_sem,
):
    me = lax.axis_index("beam")
    unit = scale_ref.shape[0]
    rows = n * unit
    width = local * tile_count
    s_vmem = grad_ref
    chunks = len(KINDS)
    wide = pixels // chunks
    block = rows // 8
    core, across, line = me % 2, me // 2 % 2, me // 4
    side = line // 2
    far = 1 - side
    inward = (1 - 2 * side) * 4
    peers = {
        "c": me + 1 - 2 * core,
        "y": me + 2 - 4 * across,
        "t": me + inward,
        "m": me + inward,
        "o": me - inward,
    }

    def columns(k):
        return pl.ds(k * wide, wide)

    loads = []
    for k in range(chunks):
        load = pltpu.make_async_copy(s_ref.at[:, columns(k)], s_vmem.at[:, columns(k)], s_sem.at[k])
        loads.append(load)
    target_load = pltpu.make_async_copy(target_hbm, target_ref, s_sem.at[chunks])
    barrier = pltpu.get_barrier_semaphore()
    for ahead in range(1, n):
        pl.semaphore_signal(
            barrier, inc=1, device_id={"beam": lax.rem(me + ahead, n)}, device_id_type=pl.DeviceIdType.MESH
        )
    target_load.start()
    for load in loads:
        load.start()
    probes = unit // 2
    raw[...] = jnp.zeros_like(raw)
    raw[0:2, 0:probes] = shift_ref[...]
    raw[2:3, 0:probes] = cutoff_ref[...]
    raw[3:4, 0:probes] = exp_ref[...]
    scale = jnp.exp2(raw[...].T[0:probes, 3:4].astype(jnp.float32))
    scale_ref[0:probes, :] = jnp.broadcast_to(scale, (probes, 128))
    scale_ref[probes:unit, :] = jnp.broadcast_to(scale, (probes, 128))
    table = raw[...]
    packed = table[0:1, :]
    for k in range(1, 4):
        packed = packed + pltpu.roll(table, k * probes, 1)[k : k + 1, :]
    par_ref[0] = packed
    pl.semaphore_wait(barrier, n - 1)

    def remote(source, target, send_semaphore, recv_semaphore, peer):
        return pltpu.make_async_remote_copy(
            src_ref=source,
            dst_ref=target,
            send_sem=send_semaphore,
            recv_sem=recv_semaphore,
            device_id={"beam": peer},
            device_id_type=pl.DeviceIdType.MESH,
        )

    pars[me] = par_ref[0]
    asked = [
        remote(par_ref.at[0], pars.at[me], par_send.at[ahead - 1], par_recv.at[ahead - 1], lax.rem(me + ahead, n))
        for ahead in range(1, n)
    ]
    for copy in asked:
        copy.start()
    for copy in asked:
        copy.wait_recv()
    for at in range(n):
        flat[at : at + 1, :] = pars[at]
    turned = flat[...].T

    def column(k):
        return jnp.concatenate([turned[k * probes : (k + 1) * probes, at : at + 1] for at in range(n)], axis=0)

    half = SIDE // 2
    beam = me * local + lax.broadcasted_iota(jnp.int32, (1, local), 1)
    freq_x = beam % SIDE - half
    freq_y = beam // SIDE - half
    shift_x = column(0)
    shift_y = column(1)
    cutoff = column(2)
    ramp = (freq_x * shift_x + freq_y * shift_y) % GRID
    phase = ramp.astype(jnp.float32) * (TWO_PI / GRID)
    inside = (freq_x * freq_x + freq_y * freq_y) <= cutoff
    cosine = jnp.cos(phase)
    sine = jnp.sin(phase)
    w_real = weight_ref[0:1, :]
    w_imag = weight_ref[1:2, :]
    c_real = jnp.where(inside, w_real * cosine + w_imag * sine, 0.0).reshape(n, probes, local)
    c_imag = jnp.where(inside, w_imag * cosine - w_real * sine, 0.0).reshape(n, probes, local)
    mix[0, :, 0] = c_real
    mix[0, :, 1] = c_imag
    mix[1, :, 0] = -c_imag
    mix[1, :, 1] = c_real
    first = mix[0].reshape(rows, local).astype(jnp.bfloat16)
    second = mix[1].reshape(rows, local).astype(jnp.bfloat16)
    step = GRID // TILE_SIDE
    window = (shift_x // step * TILE_SIDE + shift_y // step).reshape(n, probes, 1)
    window = jnp.concatenate([window, window], axis=1).reshape(rows, 1)
    place_of = lax.broadcasted_iota(jnp.int32, (1, width), 1)
    chosen = window == place_of % tile_count
    spread = lax.broadcasted_iota(jnp.int32, (local, width), 1) // tile_count
    spread = (spread == lax.broadcasted_iota(jnp.int32, (local, width), 0)).astype(jnp.float32).astype(jnp.bfloat16)
    for at, part in ((0, first), (width, second)):
        full = jnp.dot(part, spread, preferred_element_type=jnp.float32)
        left_ref[:, at : at + width] = jnp.where(chosen, full, 0.0).astype(jnp.bfloat16)
    parts[0] = first
    parts[1] = second
    target_load.wait()

    def turn(part):
        window_row = jnp.broadcast_to(window.astype(jnp.float32), (rows, 128)).T[0:1, :]
        tile = lax.broadcasted_iota(jnp.int32, (width, 1), 0) % tile_count
        beams = lax.broadcasted_iota(jnp.int32, (width, local), 0) // tile_count
        beams = (beams == lax.broadcasted_iota(jnp.int32, (width, local), 1)).astype(jnp.float32).astype(jnp.bfloat16)
        full = lax.dot_general(beams, parts[part], (((1,), (1,)), ((), ())), preferred_element_type=jnp.float32)
        chosen_row = tile.astype(jnp.float32) == window_row
        turned_ref[part * width : (part + 1) * width, :] = jnp.where(chosen_row, full, 0.0).astype(jnp.bfloat16)

    own = (me * unit // block // 4, me * unit // block // 2 % 2, me * unit // block % 2)
    own_rows = pl.ds(pl.multiple_of(me * unit % block, unit), unit)

    def run(inner, steps):
        sent = []

        def send(k, link, message, source, target):
            copy = remote(
                source, target, send_sem.at[k, len([1 for other, _ in sent if other == k])],
                recv_sem.at[k, NAMES.index(message)], peers[link],
            )
            copy.start()
            sent.append((k, copy))

        def got(k, message, view):
            remote(view, view, send_sem.at[k, 0], recv_sem.at[k, NAMES.index(message)], peers["c"]).wait_recv()

        def low(x):
            return x.astype(jnp.bfloat16)

        def spread_first(k):
            held = res_ref.at[k, core, across, side]
            if KINDS[k][1] == "Y":
                send(k, "m", "gf1", held, held)
                send(k, "o", "gn1", held, held)
                send(k, "y", "ga", held, held)
            else:
                send(k, "y", "ga", held, held)
                send(k, "m", "gf1", held, held)
                send(k, "o", "gn1", held, held)

        def take(k, name):
            by_y = KINDS[k][0] == "Y"
            at = (k, core, across)
            here = (k, core, across, side)
            if name == "M":
                loads[k].wait()
                product = jnp.dot(left_ref[...], s_vmem[:, columns(k)], preferred_element_type=jnp.float32)
                acc[k] = product.reshape(2, 2, 2, block, wide)
                goal = target_ref[:, columns(k)].astype(jnp.float32) * scale_ref[:, 0:1]
                acc[(k, *own, own_rows)] = acc[(k, *own, own_rows)] - goal
                sbuf[k, 1 - core] = low(acc[k, 1 - core])
                send(k, "c", "r1", sbuf.at[k, 1 - core], r1.at[k])
            elif name == "C":
                got(k, "r1", r1.at[k])
                if by_y:
                    sbuf[k, core, 1 - across] = low(acc[k, core, 1 - across] + r1[k, 1 - across].astype(jnp.float32))
                    send(k, "y", "r2", sbuf.at[k, core, 1 - across], r2.at[k])
                    acc[at] = acc[at] + r1[k, across].astype(jnp.float32)
                elif inner:
                    acc[k, core] = acc[k, core] + r1[k].astype(jnp.float32)
                else:
                    for at_side, message, slot in ((far, "r3f", 0), (side, "r3n", 1)):
                        total = acc[k, core, :, at_side] + r1[k, :, at_side].astype(jnp.float32)
                        sbuf[k, core, :, at_side] = low(total)
                        send(k, "t", message, sbuf.at[k, core, :, at_side], r3.at[k, slot])
            elif name == "Y":
                if by_y:
                    got(k, "r2", r2.at[k])
                    total = acc[at] + r2[k].astype(jnp.float32)
                    if inner:
                        acc[at] = total
                    else:
                        sbuf[at] = low(total)
                        send(k, "t", "r3f", sbuf.at[(*at, far)], r3.at[k, 0, 0])
                        send(k, "t", "r3n", sbuf.at[(*at, side)], r3.at[k, 1, 0])
                else:
                    got(k, "r2", r2.at[k, 0])
                    res_ref[here] = low(acc[here] + r2[k, 0].astype(jnp.float32))
                    spread_first(k)
            elif name == "F":
                if by_y:
                    got(k, "r3f", r3.at[k, 0, 0])
                    sbuf[(*at, far)] = low(acc[(*at, far)] + r3[k, 0, 0].astype(jnp.float32))
                    send(k, "m", "r4", sbuf.at[(*at, far)], r4.at[k, 0])
                else:
                    got(k, "r3f", r3.at[k, 0])
                    sbuf[k, core, :, far] = low(acc[k, core, :, far] + r3[k, 0].astype(jnp.float32))
                    send(k, "m", "r4", sbuf.at[k, core, :, far], r4.at[k])
            elif name == "N":
                if by_y:
                    got(k, "r3n", r3.at[k, 1, 0])
                    got(k, "r4", r4.at[k, 0])
                    total = acc[here] + r3[k, 1, 0].astype(jnp.float32) + r4[k, 0].astype(jnp.float32)
                    res_ref[here] = low(total)
                    spread_first(k)
                else:
                    got(k, "r3n", r3.at[k, 1])
                    got(k, "r4", r4.at[k])
                    there = (k, core, 1 - across, side)
                    total = acc[there] + r3[k, 1, 1 - across].astype(jnp.float32) + r4[k, 1 - across].astype(jnp.float32)
                    sbuf[there] = low(total)
                    send(k, "y", "r2", sbuf.at[there], r2.at[k, 0])
                    acc[here] = acc[here] + r3[k, 1, across].astype(jnp.float32) + r4[k, across].astype(jnp.float32)
            elif name == "A":
                if KINDS[k][1] == "Y":
                    got(k, "ga", res_ref.at[here])
                    got(k, "gb", res_ref.at[here])
                elif inner:
                    got(k, "gf2", res_ref.at[here])
                    held = res_ref.at[k, core, 1 - across, far]
                    send(k, "o", "gf2", held, held)
                else:
                    for message in ("gn1", "gn2", "gf1", "gf2"):
                        got(k, message, res_ref.at[here])
                send(k, "c", "ac", res_ref.at[k, core], res_ref.at[k, core])
            elif name == "H":
                got(k, "ga", res_ref.at[here])
                held = res_ref.at[k, core, 1 - across, side]
                send(k, "m", "gf2", held, held)
                send(k, "o", "gn2", held, held)
            elif name == "G1":
                if inner:
                    got(k, "gf1", res_ref.at[here])
                    held = res_ref.at[(*at, far)]
                    send(k, "o", "gf1", held, held)
                    if KINDS[k][1] == "Y":
                        send(k, "y", "gb", held, held)
                else:
                    got(k, "gn1", res_ref.at[here])
                    held = res_ref.at[here]
                    send(k, "y", "ga", held, held)
            elif name == "G2":
                got(k, "gf1", res_ref.at[here])
                held = res_ref.at[(*at, far)]
                send(k, "y", "gb", held, held)
            elif name == "E":
                got(k, "ac", res_ref.at[k, 1 - core])
            elif name in ("P0", "P1"):
                tall = width // 2

                def part_of(i, carry):
                    at = pl.ds(pl.multiple_of((2 * int(name[1]) + i) * tall, tall), tall)
                    held = res_ref[k].reshape(rows, wide)
                    grad_ref[at, columns(k)] = low(jnp.dot(turned_ref[at, :], held, preferred_element_type=jnp.float32))
                    return carry

                lax.fori_loop(0, 2, part_of, 0)
            elif name in ("T0", "T1"):
                turn(int(name[1]))

        for k, name in steps:
            take(k, name)
        for _, copy in sent:
            copy.wait_send()

    edge_steps, inner_steps = schedule(block * wide * 2)
    middle = (line == 1) | (line == 2)

    @pl.when(middle)
    def _():
        run(True, inner_steps)

    @pl.when(jnp.logical_not(middle))
    def _():
        run(False, edge_steps)

    for copy in asked:
        copy.wait_send()


def stage_strides(n):
    return [2**k for k in range(n.bit_length() - 1)]


def orders(n):
    strides = stage_strides(n)
    other = list(strides)
    if SWAP and len(other) > 2:
        other[1], other[2] = other[2], other[1]
    return strides, other


def place(me, strides, unit, upto):
    levels = len(strides)
    base = 0
    for k in range(upto):
        base = base + (me // strides[k]) % 2 * (unit * 2 ** (levels - 1 - k))
    return base


def wave_kernel(
    n, local, tile_count, pixels, strides, other,
    par_ref, weight_ref, target_ref, s_ref,
    res_ref, left_ref,
    pars, s_vmem, acc, sbuf, rbuf, mixed_left, mixed_res,
    par_send, par_recv, s_sem, send_sem, recv_sem,
):
    levels = len(strides)
    me = lax.axis_index("beam")
    unit = par_ref.shape[0]
    rows = n * unit
    width = local * tile_count
    wide = pixels // CHUNKS

    def order(c):
        return other if c % 2 else strides

    moves = [(place(i, other, unit, levels), place(i, strides, unit, levels)) for i in range(n)]

    def partner(stride):
        return me + (1 - 2 * ((me // stride) % 2)) * stride

    def columns(c):
        return pl.ds(c * wide, wide)

    loads = []
    for c in range(CHUNKS):
        load = pltpu.make_async_copy(s_ref.at[:, columns(c)], s_vmem.at[:, columns(c)], s_sem.at[c])
        load.start()
        loads.append(load)

    barrier = pltpu.get_barrier_semaphore()
    for ahead in range(1, n):
        pl.semaphore_signal(
            barrier, inc=1, device_id={"beam": lax.rem(me + ahead, n)}, device_id_type=pl.DeviceIdType.MESH
        )
    pl.semaphore_wait(barrier, n - 1)

    sent = []

    def send(source, target, send_semaphore, recv_semaphore, peer):
        copy = pltpu.make_async_remote_copy(
            src_ref=source,
            dst_ref=target,
            send_sem=send_semaphore,
            recv_sem=recv_semaphore,
            device_id={"beam": peer},
            device_id_type=pl.DeviceIdType.MESH,
        )
        copy.start()
        sent.append(copy)
        return copy

    def mine(k, steps=strides):
        size = unit * 2 ** (levels - k)
        return pl.ds(pl.multiple_of(place(me, steps, unit, k), size), size)

    pars[mine(levels), :] = par_ref[...]
    asked = [
        send(par_ref, pars.at[mine(levels), :], par_send.at[ahead - 1], par_recv.at[ahead - 1], lax.rem(me + ahead, n))
        for ahead in range(1, n)
    ]
    for copy in asked:
        copy.wait_recv()

    half = SIDE // 2
    beam = me * local + lax.broadcasted_iota(jnp.int32, (1, local), 1)
    freq_x = beam % SIDE - half
    freq_y = beam // SIDE - half
    shift_x = pars[:, 0:1]
    shift_y = pars[:, 1:2]
    cutoff = pars[:, 2:3]
    ramp = (freq_x * shift_x + freq_y * shift_y) % GRID
    phase = ramp.astype(jnp.float32) * (TWO_PI / GRID)
    inside = (freq_x * freq_x + freq_y * freq_y) <= cutoff
    cosine = jnp.cos(phase)
    sine = jnp.sin(phase)
    w_real = weight_ref[0:1, :]
    w_imag = weight_ref[1:2, :]
    c_real = jnp.where(inside, w_real * cosine + w_imag * sine, 0.0)
    c_imag = jnp.where(inside, w_imag * cosine - w_real * sine, 0.0)
    is_real = lax.broadcasted_iota(jnp.int32, (rows, 1), 0) % unit < unit // 2
    first = jnp.where(is_real, c_real, c_imag).astype(jnp.bfloat16)
    second = jnp.where(is_real, -c_imag, c_real).astype(jnp.bfloat16)
    step = GRID // TILE_SIDE
    window = shift_x // step * TILE_SIDE + shift_y // step
    place_of = lax.broadcasted_iota(jnp.int32, (1, width), 1)
    chosen = window == place_of % tile_count
    spread = lax.broadcasted_iota(jnp.int32, (local, width), 1) // tile_count
    spread = (spread == lax.broadcasted_iota(jnp.int32, (local, width), 0)).astype(jnp.float32).astype(jnp.bfloat16)
    for at, part in ((0, first), (width, second)):
        full = jnp.dot(part, spread, preferred_element_type=jnp.float32)
        left_ref[:, at : at + width] = jnp.where(chosen, full, 0.0).astype(jnp.bfloat16)

    if other != strides:
        for at, old in moves:
            mixed_left[at : at + unit, :] = left_ref[old : old + unit, :]

    def left_of(c):
        return left_ref if order(c) == strides else mixed_left

    def res_of(c):
        return res_ref if order(c) == strides else mixed_res

    narrow = min(MATMUL_COLUMNS, wide)

    def multiply(c):
        def tile(i, carry):
            at = pl.ds(pl.multiple_of(c * wide + i * narrow, narrow), narrow)
            acc[:, at] = jnp.dot(left_of(c)[...], s_vmem[:, at], preferred_element_type=jnp.float32)
            return carry

        lax.fori_loop(0, wide // narrow, tile, 0)

    def scatter_rows(c, k):
        size = rows // 2 ** (k + 1)
        base = place(me, order(c), unit, k)
        bit = (me // order(c)[k]) % 2
        keep = pl.ds(pl.multiple_of(base + bit * size, size), size)
        give = pl.ds(pl.multiple_of(base + (1 - bit) * size, size), size)
        slot = pl.ds(rows - 2 * size, size)
        return keep, give, slot

    def start_scatter(c, k):
        _, give, slot = scatter_rows(c, k)
        sbuf[slot, columns(c)] = acc[give, columns(c)].astype(jnp.bfloat16)
        return send(
            sbuf.at[slot, columns(c)],
            rbuf.at[slot, columns(c)],
            send_sem.at[c, k],
            recv_sem.at[c, k],
            partner(order(c)[k]),
        )

    def end_scatter(c, k):
        keep, _, slot = scatter_rows(c, k)
        acc[keep, columns(c)] += rbuf[slot, columns(c)].astype(jnp.float32)

    def residual(c):
        own = mine(levels, order(c))
        scale = jnp.exp2(par_ref[:, 3:4].astype(jnp.float32))
        goal = target_ref[:, columns(c)].astype(jnp.float32) * scale
        res_of(c)[own, columns(c)] = (acc[own, columns(c)] - goal).astype(jnp.bfloat16)

    def start_gather(c, k):
        held = res_of(c).at[mine(k + 1, order(c)), columns(c)]
        at = 2 * levels - 1 - k
        return send(held, held, send_sem.at[c, at], recv_sem.at[c, at], partner(order(c)[k]))

    def slots(c):
        hops = order(c) + order(c)[::-1]
        taken = [0]
        for stride in hops:
            taken.append(taken[-1] + (GAP_NEAR if stride == 1 else GAP_FAR))
        return taken

    flight = {}
    for time in range(CHUNKS + slots(0)[-1]):
        for c in range(CHUNKS):
            if time - c not in slots(c):
                continue
            at = slots(c).index(time - c)
            if at == 0:
                loads[c].wait()
                multiply(c)
            else:
                flight[c].wait_recv()
                if at <= levels:
                    end_scatter(c, at - 1)
            if at < levels:
                flight[c] = start_scatter(c, at)
            elif at < 2 * levels:
                if at == levels:
                    residual(c)
                flight[c] = start_gather(c, 2 * levels - 1 - at)
    for c in range(CHUNKS):
        if order(c) != strides:
            for at, old in moves:
                res_ref[old : old + unit, columns(c)] = mixed_res[at : at + unit, columns(c)]
    for copy in sent:
        copy.wait_send()


def grad_kernel(left_ref, res_ref, out_ref):
    dims = (((0,), (0,)), ((), ()))
    out_ref[...] = lax.dot_general(left_ref[...], res_ref[...], dims, preferred_element_type=jnp.float32).astype(
        out_ref.dtype
    )


def finish_kernel(done_ref, turned_ref, res_ref, out_ref, last, sem):
    height = turned_ref.shape[0]
    chunks, _, wide = res_ref.shape
    ready = out_ref.shape[1] - wide * LATE
    tall = height // 4
    copies = []
    for i in range(4):
        at = pl.ds(i * tall, tall)
        copies.append(pltpu.make_async_copy(done_ref.at[at, pl.ds(0, ready)], out_ref.at[at, pl.ds(0, ready)], sem.at[i]))
        copies[-1].start()
    for i in range(4):
        at = pl.ds(i * tall, tall)
        for k in range(LATE):
            held = res_ref[chunks - LATE + k]
            product = jnp.dot(turned_ref[at, :], held, preferred_element_type=jnp.float32)
            last[at, k * wide : (k + 1) * wide] = product.astype(jnp.bfloat16)
        copies.append(pltpu.make_async_copy(last.at[at, :], out_ref.at[at, pl.ds(ready, wide * LATE)], sem.at[4 + i]))
        copies[-1].start()
    for copy in copies:
        copy.wait()


def grid_body(n, s_matrix, beam_weight, probe_shift, probe_cutoff, target, target_exp):
    _, local, tile_count, pixels = s_matrix.shape
    probes = probe_shift.shape[0]
    unit = 2 * probes
    rows = n * unit
    block = rows // 8
    width = local * tile_count
    chunks = len(KINDS)
    wide = pixels // chunks
    vmem = pl.BlockSpec(memory_space=pltpu.VMEM)
    hbm = pl.BlockSpec(memory_space=pl.ANY)
    done, res, turned = pl.pallas_call(
        functools.partial(grid_kernel, n, local, tile_count, pixels),
        out_shape=(
            pltpu.VMEM((2 * width, pixels), jnp.bfloat16),
            pltpu.VMEM((chunks, 2, 2, 2, block, wide), jnp.bfloat16),
            pltpu.VMEM((2 * width, rows), jnp.bfloat16),
        ),
        in_specs=[vmem, vmem, vmem, vmem, hbm, hbm],
        out_specs=(vmem, vmem, vmem),
        scratch_shapes=[
            pltpu.VMEM((8, 128), jnp.int32),
            pltpu.VMEM((1, 1, 128), jnp.int32),
            pltpu.VMEM((unit, 128), jnp.float32),
            pltpu.VMEM((n, 128), jnp.int32),
            pltpu.VMEM((2, n, 2, probes, local), jnp.float32),
            pltpu.VMEM((unit, pixels), jnp.bfloat16),
            pltpu.VMEM((2, rows, local), jnp.bfloat16),
            pltpu.VMEM((rows, 2 * width), jnp.bfloat16),
            pltpu.VMEM((n, 1, 128), jnp.int32),
            pltpu.VMEM((chunks, 2, 2, 2, block, wide), jnp.float32),
            pltpu.VMEM((chunks, 2, 2, 2, block, wide), jnp.bfloat16),
            pltpu.VMEM((chunks, 2, 2, block, wide), jnp.bfloat16),
            pltpu.VMEM((chunks, 2, block, wide), jnp.bfloat16),
            pltpu.VMEM((chunks, 2, 2, block, wide), jnp.bfloat16),
            pltpu.VMEM((chunks, 2, block, wide), jnp.bfloat16),
            pltpu.SemaphoreType.DMA((n - 1,)),
            pltpu.SemaphoreType.DMA((n - 1,)),
            pltpu.SemaphoreType.DMA((chunks + 1,)),
            pltpu.SemaphoreType.DMA((chunks, 12)),
            pltpu.SemaphoreType.DMA((chunks, len(NAMES))),
        ],
        compiler_params=pltpu.CompilerParams(
            collective_id=0, has_side_effects=True, vmem_limit_bytes=36 * 2**20
        ),
    )(
        probe_shift.T, probe_cutoff.reshape(1, probes), target_exp.reshape(1, probes), beam_weight,
        target.reshape(unit, pixels), s_matrix.reshape(2 * width, pixels),
    )
    grad = pl.pallas_call(
        finish_kernel,
        out_shape=jax.ShapeDtypeStruct((2 * width, pixels), jnp.bfloat16),
        in_specs=[vmem, vmem, vmem],
        out_specs=hbm,
        scratch_shapes=[pltpu.VMEM((2 * width, wide * LATE), jnp.bfloat16), pltpu.SemaphoreType.DMA((8,))],
        compiler_params=pltpu.CompilerParams(vmem_limit_bytes=8 * 2**20),
    )(done, turned, res.reshape(chunks, rows, wide))
    return grad.reshape(2, local, tile_count, pixels)


def body(n, s_matrix, beam_weight, probe_shift, probe_cutoff, target, target_exp):
    if n == 16 and probe_shift.shape[0] == 8:
        return grid_body(n, s_matrix, beam_weight, probe_shift, probe_cutoff, target, target_exp)
    _, local, tile_count, pixels = s_matrix.shape
    probes = probe_shift.shape[0]
    strides, other = orders(n)
    levels = len(strides)
    unit = 2 * probes
    rows = n * unit
    width = local * tile_count
    pars = jnp.concatenate([probe_shift, probe_cutoff[:, None], target_exp[:, None]], axis=1)
    pars = jnp.pad(jnp.concatenate([pars, pars], axis=0), ((0, 0), (0, 124)))
    vmem = pl.BlockSpec(memory_space=pltpu.VMEM)
    res, left = pl.pallas_call(
        functools.partial(wave_kernel, n, local, tile_count, pixels, strides, other),
        out_shape=(
            jax.ShapeDtypeStruct((rows, pixels), jnp.bfloat16),
            jax.ShapeDtypeStruct((rows, 2 * width), jnp.bfloat16),
        ),
        in_specs=[vmem, vmem, vmem, pl.BlockSpec(memory_space=pl.ANY)],
        out_specs=(vmem, vmem),
        scratch_shapes=[
            pltpu.VMEM((rows, 128), jnp.int32),
            pltpu.VMEM((2 * width, pixels), jnp.bfloat16),
            pltpu.VMEM((rows, pixels), jnp.float32),
            pltpu.VMEM((rows, pixels), jnp.bfloat16),
            pltpu.VMEM((rows, pixels), jnp.bfloat16),
            pltpu.VMEM((rows, 2 * width), jnp.bfloat16),
            pltpu.VMEM((rows, pixels), jnp.bfloat16),
            pltpu.SemaphoreType.DMA((n - 1,)),
            pltpu.SemaphoreType.DMA((n - 1,)),
            pltpu.SemaphoreType.DMA((CHUNKS,)),
            pltpu.SemaphoreType.DMA((CHUNKS, 2 * levels)),
            pltpu.SemaphoreType.DMA((CHUNKS, 2 * levels)),
        ],
        compiler_params=pltpu.CompilerParams(
            collective_id=0, has_side_effects=True, vmem_limit_bytes=60 * 2**20
        ),
    )(pars, beam_weight, target.reshape(unit, pixels), s_matrix.reshape(2 * width, pixels))
    tall = min(512, width)
    grad = pl.pallas_call(
        grad_kernel,
        grid=(2 * width // tall,),
        out_shape=jax.ShapeDtypeStruct((2 * width, pixels), jnp.bfloat16),
        in_specs=[
            pl.BlockSpec((rows, tall), lambda i: (0, i)),
            pl.BlockSpec((rows, pixels), lambda i: (0, 0)),
        ],
        out_specs=pl.BlockSpec((tall, pixels), lambda i: (i, 0)),
        compiler_params=pltpu.CompilerParams(vmem_limit_bytes=60 * 2**20),
    )(left, res)
    return grad.reshape(2, local, tile_count, pixels)


def solution(mesh):
    return jax.shard_map(
        functools.partial(body, mesh.shape["beam"]),
        mesh=mesh,
        in_specs=(
            P(None, ("grp", "beam"), None, None),
            P(None, ("grp", "beam")),
            P(("grp", "beam"), None),
            P(("grp", "beam")),
            P(None, ("grp", "beam"), None),
            P(("grp", "beam")),
        ),
        out_specs=P(None, ("grp", "beam"), None, None),
        check_vma=False,
    )
```
